512 devices in a mesh: frame: 16 (over z), row: 16 (over x, y_hi, core), dp: 2 (over y_lo).
Axes of the slice: x: 4, y: 4 (y_hi: 2, y_lo: 2; y = y_hi * 2 + y_lo), z: 16, core: 2. Of those that a mesh axis runs over, the one named last changes fastest.
Arguments:
- queries: bfloat16 [32, 48, 80, 2048], P(('dp', 'frame'), None, None, 'row'), parts along dimension 0, may hold values from -24 to 24
- keys: bfloat16 [32, 48, 80, 2048], P(('dp', 'frame'), None, None, 'row'), parts along dimension 0, may hold values from -6 to 6
- values: bfloat16 [32, 48, 80, 2048], P(('dp', 'frame'), None, None, 'row'), parts along dimension 0, may hold values from -6 to 6
- back_reach: int32 [12, 10], P('dp'), parts along dimension 0, may hold values from 0 to 15
- fwd_reach: int32 [12, 10], P('dp'), parts along dimension 0, may hold values from 0 to 15
- valid_rows: int32 [32], P('dp'), parts along dimension 0, may hold values from 41 to 48
- valid_cols: int32 [32], P('dp'), parts along dimension 0, may hold values from 73 to 80
Outputs:
- block_out: bfloat16 [32, 48, 80, 2048], P(('dp', 'frame'), None, None, 'row'), parts along dimension 0
The draws below stay inside these ranges and needn't reach their ends.
There are 2 independent parts, one for each index of `dp`. The reference program is written for one: setup_inputs(seed, part) draws one part's arguments, and reference() takes and returns one part's arrays. A program takes and returns all parts, laid end to end along the dimension named above; each array names one. Nothing has to cross between parts.
All inputs are finite; a program needn't handle non-finite values.
Results may differ from the reference program's by a relative error of at most 0.012.
Values may be sent and summed in bfloat16 or wider, within the bound.
A program may use at most 64 MiB of HBM per device.

```python
import math
import jax
import jax.numpy as jnp
from jax import lax

HEADS = 16
DH = 128
TS = 8
NTR = 6
TC = 10
NF = 16
HT = 48
WT = 80


def shared_keys(key):
    return jnp.clip(jax.random.normal(jax.random.fold_in(key, 11), (NF, HT, WT, HEADS * DH), jnp.float32), -6.0, 6.0)


def draw_keys(key, part):
    return shared_keys(key).astype(jnp.bfloat16)


def draw_queries(key, part):
    full_shape = (NF, HT, WT, HEADS * DH)
    drawn = jax.random.normal(jax.random.fold_in(key, 23), full_shape, jnp.float32)
    return jnp.clip(drawn, -6.0, 6.0).astype(jnp.bfloat16)


def place_ends(entries, stream_key, low, top_value):
    spot = [jax.random.randint(jax.random.fold_in(stream_key, axis), (), 0, length) for axis, length in enumerate(entries.shape)]
    longest = entries.shape.index(max(entries.shape))
    neighbour = spot[:longest] + [(spot[longest] + 1) % entries.shape[longest]] + spot[longest + 1:]
    return entries.at[tuple(spot)].set(low).at[tuple(neighbour)].set(top_value)


def block_levels(rng, extent, shards, least, top_value):
    gain, own = 1.0, jax.random.fold_in(rng, 6)
    for dim, shards_of in shards:
        steps = jnp.exp(jax.random.uniform(jax.random.fold_in(own, dim), (shards_of,), jnp.float32, least / len(shards), top_value / len(shards)))
        gain = gain * jnp.repeat(steps, extent[dim] // shards_of).reshape([-1 if axis == dim else 1 for axis in range(len(extent))])
    return gain


def gaussian(rng, dims, width, limit, shards=(), held_as=jnp.bfloat16):
    result = jax.random.normal(rng, dims, jnp.float32) * width
    if len(shards) > 0:
        result = block_levels(rng, dims, shards, -0.22, 0.18) * result
    return jnp.clip(result, min=-limit, max=limit).astype(held_as)


def setup_inputs(seed: int = 0, part: int = 0) -> dict:
    seeds = jax.random.split(jax.random.key(seed), 8)
    part_keys = jax.random.split(jax.random.fold_in(seeds[7], part), 8)
    queries = draw_queries(jax.random.fold_in(jax.random.fold_in(seeds[7], part), 71), part)
    keys = draw_keys(jax.random.fold_in(jax.random.fold_in(seeds[7], part), 71), part)
    values = gaussian(part_keys[2], (NF, HT, WT, HEADS * DH), 1.0, 6.0, ((0, 16), (3, 16)))
    back_reach = place_ends(jax.random.randint(part_keys[3], (NTR, TC), 0, NF), jax.random.fold_in(part_keys[3], 1), 0, NF - 1).astype(jnp.int32)
    fwd_reach = place_ends(jax.random.randint(part_keys[4], (NTR, TC), 0, NF), jax.random.fold_in(part_keys[4], 1), 0, NF - 1).astype(jnp.int32)
    valid_rows = place_ends(jax.random.randint(part_keys[5], (NF,), HT - TS + 1, HT + 1), jax.random.fold_in(part_keys[5], 1), HT - TS + 1, HT).astype(jnp.int32)
    valid_cols = place_ends(jax.random.randint(part_keys[6], (NF,), WT - TS + 1, WT + 1), jax.random.fold_in(part_keys[6], 1), WT - TS + 1, WT).astype(jnp.int32)
    return {"queries": queries, "keys": keys, "values": values, "back_reach": back_reach, "fwd_reach": fwd_reach, "valid_rows": valid_rows, "valid_cols": valid_cols}


def attend(query_rows, key_rows, value_rows, allowed):
    dot_terms = jnp.dot(query_rows, key_rows.T, preferred_element_type=jnp.float32)
    query_sq = lax.optimization_barrier(jnp.sum(jnp.square(query_rows.astype(jnp.float32)), axis=1))
    key_sq = lax.optimization_barrier(jnp.sum(jnp.square(key_rows.astype(jnp.float32)), axis=1))
    distance = query_sq[:, None] + key_sq[None, :] - 2.0 * dot_terms
    scores = jnp.where(allowed, -distance * (0.5 / math.sqrt(query_rows.shape[1])), -jnp.inf)
    highest = lax.optimization_barrier(jnp.max(scores, axis=1, keepdims=True))
    weights = jnp.exp(scores - highest)
    totals = lax.optimization_barrier(jnp.sum(weights, axis=1, keepdims=True))
    mixed = jnp.dot(weights.astype(jnp.bfloat16), value_rows, preferred_element_type=jnp.float32)
    return mixed / totals

def tile_split(block):
    frames = block.shape[0]
    heads = block.shape[3] // DH
    return block.reshape(frames, NTR, TS, TC, TS, heads, DH).transpose(5, 0, 1, 3, 2, 4, 6).reshape(heads, frames, NTR * TC, TS * TS, DH)

def neighbours(tiles):
    count = tiles.shape[0]
    grid = tiles.reshape((count, NTR, TC) + tiles.shape[2:])
    padded = jnp.pad(grid, ((0, 0), (1, 1), (1, 1), (0, 0), (0, 0)))
    views = [padded[:, dy:dy + NTR, dx:dx + TC] for dy in range(3) for dx in range(3)]
    stacked = jnp.stack(views, axis=3)
    return stacked.reshape(count * NTR * TC, 9 * tiles.shape[2], tiles.shape[3])

def reference(queries, keys, values, back_reach, fwd_reach, valid_rows, valid_cols):
    tile_area = TS * TS
    count_tiles = NTR * TC
    row_ids = jnp.arange(HT, dtype=jnp.int32)
    col_ids = jnp.arange(WT, dtype=jnp.int32)
    row_ok = row_ids[None, :] < valid_rows[:, None]
    col_ok = col_ids[None, :] < valid_cols[:, None]
    token_valid = row_ok[:, :, None] & col_ok[:, None, :]
    tile_valid = token_valid.reshape(NF, NTR, TS, TC, TS).transpose(0, 1, 3, 2, 4).reshape(NF, NTR, TC, tile_area)
    padded_valid = jnp.pad(tile_valid, ((0, 0), (1, 1), (1, 1), (0, 0)))
    near_valid = jnp.stack([padded_valid[:, dy:dy + NTR, dx:dx + TC] for dy in range(3) for dx in range(3)], axis=3)
    near_valid = near_valid.reshape(NF, count_tiles, 1, 9 * tile_area)
    query_factor = tile_valid.reshape(NF, count_tiles, tile_area).astype(jnp.float32)
    query_t = tile_split(queries)
    key_t = tile_split(keys)
    value_t = tile_split(values)

    def spatial_frame(frame_index):
        frame_q = lax.dynamic_index_in_dim(query_t, frame_index, 1, keepdims=False)
        frame_k = lax.dynamic_index_in_dim(key_t, frame_index, 1, keepdims=False)
        frame_v = lax.dynamic_index_in_dim(value_t, frame_index, 1, keepdims=False)
        frame_mask = lax.dynamic_index_in_dim(near_valid, frame_index, 0, keepdims=False)
        frame_factor = lax.dynamic_index_in_dim(query_factor, frame_index, 0, keepdims=False)
        near_k = neighbours(frame_k)
        near_v = neighbours(frame_v)
        flat_q = frame_q.reshape(HEADS * count_tiles, tile_area, DH)
        masks = jnp.broadcast_to(frame_mask[None], (HEADS, count_tiles, 1, 9 * tile_area)).reshape(HEADS * count_tiles, 1, 9 * tile_area)
        mixed = jax.vmap(attend)(flat_q, near_k, near_v, masks).reshape(HEADS, count_tiles, tile_area, DH)
        return (mixed * frame_factor[None, :, :, None]).astype(jnp.bfloat16)
    spatial_t = lax.map(spatial_frame, jnp.arange(NF, dtype=jnp.int32)).transpose(1, 0, 2, 3, 4)
    length = NF * tile_area
    frame_of = jnp.arange(length, dtype=jnp.int32) // tile_area
    frame_gap = frame_of[None, :] - frame_of[:, None]
    back_flat = back_reach.reshape(count_tiles)
    fwd_flat = fwd_reach.reshape(count_tiles)
    valid_flat = tile_valid.reshape(NF, count_tiles, tile_area).transpose(1, 0, 2).reshape(count_tiles, length)

    def temporal_tile(tile_index):
        tile_q = lax.dynamic_index_in_dim(query_t, tile_index, 2, keepdims=False).reshape(HEADS, length, DH)
        tile_k = lax.dynamic_index_in_dim(key_t, tile_index, 2, keepdims=False).reshape(HEADS, length, DH)
        tile_v = lax.dynamic_index_in_dim(spatial_t, tile_index, 2, keepdims=False).reshape(HEADS, length, DH)
        key_ok = lax.dynamic_index_in_dim(valid_flat, tile_index, 0, keepdims=False)
        back_one = lax.dynamic_index_in_dim(back_flat, tile_index, 0, keepdims=False)
        fwd_one = lax.dynamic_index_in_dim(fwd_flat, tile_index, 0, keepdims=False)
        allowed = (frame_gap >= -back_one) & (frame_gap <= fwd_one) & key_ok[None, :]
        mixed = jax.vmap(attend, in_axes=(0, 0, 0, None))(tile_q, tile_k, tile_v, allowed)
        return mixed.astype(jnp.bfloat16)
    temporal = lax.map(temporal_tile, jnp.arange(count_tiles, dtype=jnp.int32))
    temporal = temporal.reshape(count_tiles, HEADS, NF, tile_area, DH).transpose(1, 2, 0, 3, 4)
    combined = (spatial_t.astype(jnp.float32) + temporal.astype(jnp.float32)) * query_factor[None, :, :, :, None]
    combined = combined.astype(jnp.bfloat16).reshape(HEADS, NF, NTR, TC, TS, TS, DH)
    return combined.transpose(1, 2, 4, 3, 5, 0, 6).reshape(NF, HT, WT, HEADS * DH)
```

```python
import math

import jax
import jax.numpy as jnp
from jax import lax
from jax.experimental import pallas as pl
from jax.experimental.pallas import tpu as pltpu
from jax.sharding import PartitionSpec as P

DH = 128
TS = 8
AREA = TS * TS
NF = 16
SLOTS = 4
WINDOW_LANE = 8
MASKED = -1e30
SCALE = math.log2(math.e) / math.sqrt(DH)
MESH = pl.DeviceIdType.MESH
NT = (((1,), (1,)), ((), ()))


def row_lane(rows):
    return (
        lax.broadcasted_iota(jnp.int32, (rows, DH), 0),
        lax.broadcasted_iota(jnp.int32, (rows, DH), 1),
    )


def token_valid(tile_row, tile_col, rows_ok, cols_ok):
    token, _ = row_lane(AREA)
    return (tile_row * TS + (token >> 3) < rows_ok) & (tile_col * TS + (token & 7) < cols_ok)


def key_bias(keys, valid):
    _, lane = row_lane(AREA)
    wide = keys.astype(jnp.float32)
    half = -0.5 * jnp.sum(wide * wide, axis=1, keepdims=True)
    high = half.astype(jnp.bfloat16).astype(jnp.float32)
    rest = half - high
    middle = rest.astype(jnp.bfloat16).astype(jnp.float32)
    low = rest - middle
    parts = jnp.where(lane == 0, high, jnp.where(lane == 1, middle, jnp.where(lane == 2, low, 0.0)))
    return jnp.where(valid, parts, jnp.where(lane == 0, MASKED, 0.0))


def softmax_parts(scores):
    highest = jnp.max(scores, axis=1, keepdims=True)
    weights = jnp.exp2((scores - highest) * SCALE)
    return weights.astype(jnp.bfloat16), jnp.sum(weights, axis=1, keepdims=True)


def kernel(
    q_hbm, k_hbm, v_hbm, back_ref, fwd_ref, rows_ref, cols_ref, out_ref,
    q_loc, k_loc, v_loc, k_pad, v_pad, b_pad, s_loc, qk_got, s_got, k_time, b_time, probs, inverse, o_buf,
    load_sem, send_sem, qk_sem, s_sem, out_sem,
):
    tile_rows, _, tile_cols = q_hbm.shape[:3]
    me = lax.axis_index("frame")
    shift = 2 * lax.rem(lax.axis_index("row"), 2)
    barrier = pltpu.get_barrier_semaphore()

    def peer(step):
        half = (step + 1) // 2
        return lax.rem(me + jnp.where(lax.rem(step, 2) == 1, half, NF - half), NF)

    def owned(slot, owner):
        label = lax.rem(owner + shift, NF)
        last = slot == SLOTS - 1
        exists = jnp.logical_not(last & (lax.rem(label, 4) == 3))
        place = jnp.where(last, label - label // 4, label)
        tile = jnp.minimum(slot * NF + place, tile_rows * tile_cols - 1)
        return exists, tile // tile_cols, lax.rem(tile, tile_cols)

    def greet(step, carry):
        pl.semaphore_signal(barrier, inc=1, device_id={"frame": peer(step)}, device_id_type=MESH)
        return carry

    lax.fori_loop(1, NF, greet, 0)

    def load(col, carry):
        for source, target in ((q_hbm, q_loc), (k_hbm, k_loc), (v_hbm, v_loc)):
            pltpu.make_async_copy(source.at[:, :, col], target.at[:, col], load_sem).start()
        return carry

    lax.fori_loop(0, tile_cols, load, 0)

    nothing = jnp.zeros((AREA, DH), jnp.bfloat16)
    _, lane = row_lane(AREA)
    outside = jnp.where(lane == 0, MASKED, 0.0).astype(jnp.bfloat16)

    def border(row, col):
        k_pad[row, col] = nothing
        v_pad[row, col] = nothing
        b_pad[row, col] = outside

    def border_col(col, carry):
        border(0, col)
        border(tile_rows + 1, col)
        return carry

    def border_row(row, carry):
        border(row, 0)
        border(row, tile_cols + 1)
        return carry

    lax.fori_loop(0, tile_cols + 2, border_col, 0)
    lax.fori_loop(1, tile_rows + 1, border_row, 0)

    pl.semaphore_wait(barrier, NF - 1)

    def send_qk(index, carry):
        slot, owner = index // NF, peer(lax.rem(index, NF))
        exists, row, col = owned(slot, owner)

        def copies():
            for part, source in ((0, q_hbm), (1, k_hbm)):
                yield part, source.at[row, :, col], qk_got.at[slot, part, me]

        @pl.when(exists & (owner != me))
        def _():
            for part, source, target in copies():
                pltpu.make_async_remote_copy(
                    src_ref=source, dst_ref=target,
                    send_sem=send_sem.at[part], recv_sem=qk_sem.at[slot],
                    device_id={"frame": owner}, device_id_type=MESH,
                ).start()

        @pl.when(exists & (owner == me))
        def _():
            for part, source, target in copies():
                pltpu.make_async_copy(source, target, qk_sem.at[slot]).start()

        return carry

    lax.fori_loop(0, SLOTS * NF, send_qk, 0)

    for _ in range(3):
        pltpu.make_async_copy(q_loc, q_loc, load_sem).wait()

    rows_here, cols_here = rows_ref[me], cols_ref[me]

    def bias_tile(tile, carry):
        row, col = tile // tile_cols, lax.rem(tile, tile_cols)
        valid = token_valid(row, col, rows_here, cols_here)
        keys = k_loc[row, col].reshape(AREA, DH)
        k_pad[row + 1, col + 1] = keys
        v_pad[row + 1, col + 1] = v_loc[row, col].reshape(AREA, DH)
        b_pad[row + 1, col + 1] = key_bias(keys, valid).astype(jnp.bfloat16)
        return carry

    lax.fori_loop(0, tile_rows * tile_cols, bias_tile, 0)

    ones = jnp.where(lane < 3, 1.0, 0.0).astype(jnp.bfloat16)

    def near(ref, row, col):
        slabs = [ref[row + dy, pl.ds(col, 3)].reshape(3 * AREA, DH) for dy in range(3)]
        return jnp.concatenate(slabs, axis=0)

    def spatial(index, carry):
        slot, owner = index // NF, peer(lax.rem(index, NF))
        exists, row, col = owned(slot, owner)

        @pl.when(exists)
        def _():
            tile = row * tile_cols + col
            query = jnp.concatenate([q_loc[row, col].reshape(AREA, DH), ones], axis=1)
            keys = jnp.concatenate([near(k_pad, row, col), near(b_pad, row, col)], axis=1)
            scores = lax.dot_general(query, keys, NT, preferred_element_type=jnp.float32)
            weights, total = softmax_parts(scores)
            mixed = jnp.dot(weights, near(v_pad, row, col), preferred_element_type=jnp.float32)
            valid = token_valid(row, col, rows_here, cols_here)
            s_loc[tile] = jnp.where(valid, mixed * (1.0 / total), 0.0).astype(jnp.bfloat16)
            target = s_got.at[slot, me]

            @pl.when(owner != me)
            def _():
                pltpu.make_async_remote_copy(
                    src_ref=s_loc.at[tile], dst_ref=target,
                    send_sem=send_sem.at[2], recv_sem=s_sem.at[slot],
                    device_id={"frame": owner}, device_id_type=MESH,
                ).start()

            @pl.when(owner == me)
            def _():
                pltpu.make_async_copy(s_loc.at[tile], target, s_sem.at[slot]).start()

        return carry

    lax.fori_loop(0, SLOTS * NF, spatial, 0)

    group = 4
    group_rows = group * AREA
    length = NF * AREA
    group_row, group_lane = row_lane(group_rows)

    def weigh(slot, carry):
        exists, row, col = owned(slot, me)

        @pl.when(exists)
        def _():
            got = qk_got.at[slot]
            pltpu.make_async_copy(got, got, qk_sem.at[slot]).wait()
            back, fwd = back_ref[row, col], fwd_ref[row, col]

            def bias_frame(frame, carry):
                valid = token_valid(row, col, rows_ref[frame], cols_ref[frame])
                keys = qk_got[slot, 1, frame].reshape(AREA, DH)
                bias = key_bias(keys, valid)
                gap = frame - (lane - WINDOW_LANE)
                window = (lane >= WINDOW_LANE) & (lane < WINDOW_LANE + NF)
                bias = jnp.where(window & ((gap < -back) | (gap > fwd)), MASKED, bias)
                k_time[frame] = keys
                b_time[frame] = bias.astype(jnp.bfloat16)
                return carry

            lax.fori_loop(0, NF, bias_frame, 0)

            def rows_of(part, carry):
                query = qk_got[slot, 0, pl.ds(part * group, group)].reshape(group_rows, DH)
                frame_lane = WINDOW_LANE + part * group + (group_row >> 6)
                marks = jnp.where((group_lane < 3) | (group_lane == frame_lane), 1.0, 0.0)
                query = jnp.concatenate([query, marks.astype(jnp.bfloat16)], axis=1)
                keys = jnp.concatenate(
                    [k_time[...].reshape(length, DH), b_time[...].reshape(length, DH)], axis=1
                )
                scores = lax.dot_general(query, keys, NT, preferred_element_type=jnp.float32)
                weights, total = softmax_parts(scores)
                probs[slot, part] = weights
                inverse[slot, part] = jnp.broadcast_to(1.0 / total, (group_rows, DH))
                return carry

            lax.fori_loop(0, NF // group, rows_of, 0)

        return carry

    lax.fori_loop(0, SLOTS, weigh, 0)

    def mix(slot, carry):
        exists, row, col = owned(slot, me)

        @pl.when(exists)
        def _():
            got = s_got.at[slot]
            pltpu.make_async_copy(got, got, s_sem.at[slot]).wait()

            def rows_of(part, carry):
                values = s_got[slot].reshape(length, DH)
                mixed = jnp.dot(probs[slot, part], values, preferred_element_type=jnp.float32)
                temporal = (mixed * inverse[slot, part]).astype(jnp.bfloat16).astype(jnp.float32)
                for inside in range(group):
                    frame = part * group + inside
                    valid = token_valid(row, col, rows_ref[frame], cols_ref[frame])
                    both = temporal[inside * AREA : (inside + 1) * AREA] + s_got[slot, frame].astype(
                        jnp.float32
                    )
                    both = jnp.where(valid, both, 0.0).astype(jnp.bfloat16)
                    o_buf[slot, frame] = both.reshape(TS, TS, DH)
                return carry

            lax.fori_loop(0, NF // group, rows_of, 0)

            def give(step, carry):
                frame = peer(step)
                pltpu.make_async_remote_copy(
                    src_ref=o_buf.at[slot, frame], dst_ref=out_ref.at[row, :, col],
                    send_sem=send_sem.at[3], recv_sem=out_sem,
                    device_id={"frame": frame}, device_id_type=MESH,
                ).start()
                return carry

            lax.fori_loop(1, NF, give, 0)
            pltpu.make_async_copy(o_buf.at[slot, me], out_ref.at[row, :, col], out_sem).start()

        return carry

    lax.fori_loop(0, SLOTS, mix, 0)

    pltpu.make_async_copy(out_ref, out_ref, out_sem).wait()
    exists, _, _ = owned(SLOTS - 1, me)

    def drain(owned_count):
        away = s_loc.at[pl.ds(0, tile_rows * tile_cols - owned_count)]
        for part in range(3):
            pltpu.make_async_copy(away, away, send_sem.at[part]).wait()
        sent = s_loc.at[pl.ds(0, owned_count * (NF - 1))]
        pltpu.make_async_copy(sent, sent, send_sem.at[3]).wait()

    @pl.when(exists)
    def _():
        drain(SLOTS)

    @pl.when(jnp.logical_not(exists))
    def _():
        drain(SLOTS - 1)


def per_device(queries, keys, values, back_reach, fwd_reach, valid_rows, valid_cols):
    _, token_rows, token_cols, _ = queries.shape
    tile_rows, tile_cols = token_rows // TS, token_cols // TS
    grid = (tile_rows, TS, tile_cols, TS, DH)
    padded = (tile_rows + 2, tile_cols + 2, AREA, DH)
    bf16 = jnp.bfloat16
    group = 4
    out = pl.pallas_call(
        kernel,
        out_shape=jax.ShapeDtypeStruct(grid, bf16),
        in_specs=[pl.BlockSpec(memory_space=pl.ANY)] * 3
        + [pl.BlockSpec(memory_space=pltpu.SMEM)] * 4,
        out_specs=pl.BlockSpec(memory_space=pl.ANY),
        scratch_shapes=[
            pltpu.VMEM((tile_rows, tile_cols, TS, TS, DH), bf16),
            pltpu.VMEM((tile_rows, tile_cols, TS, TS, DH), bf16),
            pltpu.VMEM((tile_rows, tile_cols, TS, TS, DH), bf16),
            pltpu.VMEM(padded, bf16),
            pltpu.VMEM(padded, bf16),
            pltpu.VMEM(padded, bf16),
            pltpu.VMEM((tile_rows * tile_cols, AREA, DH), bf16),
            pltpu.VMEM((SLOTS, 2, NF, TS, TS, DH), bf16),
            pltpu.VMEM((SLOTS, NF, AREA, DH), bf16),
            pltpu.VMEM((NF, AREA, DH), bf16),
            pltpu.VMEM((NF, AREA, DH), bf16),
            pltpu.VMEM((SLOTS, NF // group, group * AREA, NF * AREA), bf16),
            pltpu.VMEM((SLOTS, NF // group, group * AREA, DH), jnp.float32),
            pltpu.VMEM((SLOTS, NF, TS, TS, DH), bf16),
            pltpu.SemaphoreType.DMA,
            pltpu.SemaphoreType.DMA((4,)),
            pltpu.SemaphoreType.DMA((SLOTS,)),
            pltpu.SemaphoreType.DMA((SLOTS,)),
            pltpu.SemaphoreType.DMA,
        ],
        compiler_params=pltpu.CompilerParams(
            collective_id=0, has_side_effects=True, vmem_limit_bytes=52 << 20
        ),
    )(
        queries.reshape(grid), keys.reshape(grid), values.reshape(grid),
        back_reach, fwd_reach, valid_rows, valid_cols,
    )
    return out.reshape(queries.shape)


def solution(mesh):
    in_specs = (
        P(("dp", "frame"), None, None, "row"),
        P(("dp", "frame"), None, None, "row"),
        P(("dp", "frame"), None, None, "row"),
        P("dp", None),
        P("dp", None),
        P("dp"),
        P("dp"),
    )
    out_specs = P(("dp", "frame"), None, None, "row")
    return jax.shard_map(
        per_device, mesh=mesh, in_specs=in_specs, out_specs=out_specs, check_vma=False
    )
```

```python
import math

import jax
import jax.numpy as jnp
from jax import lax
from jax.experimental import pallas as pl
from jax.experimental.pallas import tpu as pltpu
from jax.sharding import PartitionSpec as P

DH = 128
TS = 8
AREA = TS * TS
NF = 16
SLOTS = 4
WINDOW_LANE = 8
MASKED = -1e30
SCALE = math.log2(math.e) / math.sqrt(DH)
MESH = pl.DeviceIdType.MESH
NT = (((1,), (1,)), ((), ()))


def row_lane(rows):
    return (
        lax.broadcasted_iota(jnp.int32, (rows, DH), 0),
        lax.broadcasted_iota(jnp.int32, (rows, DH), 1),
    )


def token_valid(tile_row, tile_col, rows_ok, cols_ok):
    token, _ = row_lane(AREA)
    return (tile_row * TS + (token >> 3) < rows_ok) & (tile_col * TS + (token & 7) < cols_ok)


def key_bias(keys, valid):
    _, lane = row_lane(AREA)
    wide = keys.astype(jnp.float32)
    half = -0.5 * jnp.sum(wide * wide, axis=1, keepdims=True)
    high = half.astype(jnp.bfloat16).astype(jnp.float32)
    rest = half - high
    middle = rest.astype(jnp.bfloat16).astype(jnp.float32)
    low = rest - middle
    parts = jnp.where(lane == 0, high, jnp.where(lane == 1, middle, jnp.where(lane == 2, low, 0.0)))
    return jnp.where(valid, parts, jnp.where(lane == 0, MASKED, 0.0))


def softmax_parts(scores):
    highest = jnp.max(scores, axis=1, keepdims=True)
    weights = jnp.exp2((scores - highest) * SCALE)
    return weights.astype(jnp.bfloat16), jnp.sum(weights, axis=1, keepdims=True)


def kernel(
    q_hbm, k_hbm, v_hbm, back_hbm, fwd_hbm, rows_hbm, cols_hbm, out_ref,
    back_ref, fwd_ref, rows_ref, cols_ref,
    q_loc, k_loc, v_loc, k_pad, v_pad, b_pad, s_loc, qk_got, s_got, k_time, b_time, probs, inverse, o_buf,
    load_sem, small_sem, stage_sem, send_sem, qk_sem, s_sem, out_sem,
):
    tile_rows, _, tile_cols = q_hbm.shape[:3]
    me = lax.axis_index("frame")
    shift = 2 * lax.rem(lax.axis_index("row"), 2)
    barrier = pltpu.get_barrier_semaphore()

    def peer(step):
        half = (step + 1) // 2
        return lax.rem(me + jnp.where(lax.rem(step, 2) == 1, half, NF - half), NF)

    def owned(slot, owner):
        label = lax.rem(owner + shift, NF)
        last = slot == SLOTS - 1
        exists = jnp.logical_not(last & (lax.rem(label, 4) == 3))
        place = jnp.where(last, label - label // 4, label)
        tile = jnp.minimum(slot * NF + place, tile_rows * tile_cols - 1)
        return exists, tile // tile_cols, lax.rem(tile, tile_cols)

    def greet(semaphore):
        for neighbour in (peer(1), peer(2)):
            pl.semaphore_signal(
                semaphore, inc=1, device_id={"frame": neighbour}, device_id_type=MESH
            )
        pl.semaphore_wait(semaphore, 2)

    small = (
        (back_hbm, back_ref), (fwd_hbm, fwd_ref), (rows_hbm, rows_ref), (cols_hbm, cols_ref)
    )
    for index, (source, target) in enumerate(small):
        pltpu.make_async_copy(source, target, small_sem.at[index]).start()

    def load(col, carry):
        for source, target in ((q_hbm, q_loc), (k_hbm, k_loc), (v_hbm, v_loc)):
            pltpu.make_async_copy(source.at[:, :, col], target.at[:, col], load_sem).start()
        return carry

    lax.fori_loop(0, tile_cols, load, 0)

    def qk_copies(slot, row, col):
        for part, source in ((0, q_hbm), (1, k_hbm)):
            yield part, source.at[row, :, col], qk_got.at[slot, part, me]

    greet(barrier)

    def send_qk(distance, carry):
        @pl.when(distance > 1)
        def _():
            greet(stage_sem.at[distance - 2])

        def send(index, carry):
            slot, side = index // 2, lax.rem(index, 2)
            owner = peer(2 * distance - 1 + side)
            exists, row, col = owned(slot, owner)

            @pl.when(exists & jnp.logical_not((distance == NF // 2) & (side == 1)))
            def _():
                for part, source, target in qk_copies(slot, row, col):
                    pltpu.make_async_remote_copy(
                        src_ref=source, dst_ref=target,
                        send_sem=send_sem.at[part], recv_sem=qk_sem.at[slot],
                        device_id={"frame": owner}, device_id_type=MESH,
                    ).start()

            return carry

        return lax.fori_loop(0, 2 * SLOTS, send, carry)

    lax.fori_loop(1, NF // 2 + 1, send_qk, 0)

    def keep_qk(slot, carry):
        exists, row, col = owned(slot, me)

        @pl.when(exists)
        def _():
            for _, source, target in qk_copies(slot, row, col):
                pltpu.make_async_copy(source, target, qk_sem.at[slot]).start()

        return carry

    lax.fori_loop(0, SLOTS, keep_qk, 0)

    nothing = jnp.zeros((AREA, DH), jnp.bfloat16)
    _, lane = row_lane(AREA)
    outside = jnp.where(lane == 0, MASKED, 0.0).astype(jnp.bfloat16)

    def border(row, col):
        k_pad[row, col] = nothing
        v_pad[row, col] = nothing
        b_pad[row, col] = outside

    def border_col(col, carry):
        border(0, col)
        border(tile_rows + 1, col)
        return carry

    def border_row(row, carry):
        border(row, 0)
        border(row, tile_cols + 1)
        return carry

    lax.fori_loop(0, tile_cols + 2, border_col, 0)
    lax.fori_loop(1, tile_rows + 1, border_row, 0)

    for _ in range(3):
        pltpu.make_async_copy(q_loc, q_loc, load_sem).wait()
    for index, (source, target) in enumerate(small):
        pltpu.make_async_copy(source, target, small_sem.at[index]).wait()

    rows_here, cols_here = rows_ref[me], cols_ref[me]

    def bias_tile(tile, carry):
        row, col = tile // tile_cols, lax.rem(tile, tile_cols)
        valid = token_valid(row, col, rows_here, cols_here)
        keys = k_loc[row, col].reshape(AREA, DH)
        k_pad[row + 1, col + 1] = keys
        v_pad[row + 1, col + 1] = v_loc[row, col].reshape(AREA, DH)
        b_pad[row + 1, col + 1] = key_bias(keys, valid).astype(jnp.bfloat16)
        return carry

    lax.fori_loop(0, tile_rows * tile_cols, bias_tile, 0)

    ones = jnp.where(lane < 3, 1.0, 0.0).astype(jnp.bfloat16)

    def near(ref, row, col):
        slabs = [ref[row + dy, pl.ds(col, 3)].reshape(3 * AREA, DH) for dy in range(3)]
        return jnp.concatenate(slabs, axis=0)

    def spatial(index, carry):
        slot, owner = index // NF, peer(lax.rem(index, NF))
        exists, row, col = owned(slot, owner)

        @pl.when(exists)
        def _():
            tile = row * tile_cols + col
            query = jnp.concatenate([q_loc[row, col].reshape(AREA, DH), ones], axis=1)
            keys = jnp.concatenate([near(k_pad, row, col), near(b_pad, row, col)], axis=1)
            scores = lax.dot_general(query, keys, NT, preferred_element_type=jnp.float32)
            weights, total = softmax_parts(scores)
            mixed = jnp.dot(weights, near(v_pad, row, col), preferred_element_type=jnp.float32)
            valid = token_valid(row, col, rows_here, cols_here)
            s_loc[tile] = jnp.where(valid, mixed * (1.0 / total), 0.0).astype(jnp.bfloat16)
            target = s_got.at[slot, me]

            @pl.when(owner != me)
            def _():
                pltpu.make_async_remote_copy(
                    src_ref=s_loc.at[tile], dst_ref=target,
                    send_sem=send_sem.at[2], recv_sem=s_sem.at[slot],
                    device_id={"frame": owner}, device_id_type=MESH,
                ).start()

            @pl.when(owner == me)
            def _():
                pltpu.make_async_copy(s_loc.at[tile], target, s_sem.at[slot]).start()

        return carry

    lax.fori_loop(0, SLOTS * NF, spatial, 0)

    group = 4
    group_rows = group * AREA
    length = NF * AREA
    group_row, group_lane = row_lane(group_rows)

    def weigh(slot, carry):
        exists, row, col = owned(slot, me)

        @pl.when(exists)
        def _():
            got = qk_got.at[slot]
            pltpu.make_async_copy(got, got, qk_sem.at[slot]).wait()
            back, fwd = back_ref[row, col], fwd_ref[row, col]

            def bias_frame(frame, carry):
                valid = token_valid(row, col, rows_ref[frame], cols_ref[frame])
                keys = qk_got[slot, 1, frame].reshape(AREA, DH)
                bias = key_bias(keys, valid)
                gap = frame - (lane - WINDOW_LANE)
                window = (lane >= WINDOW_LANE) & (lane < WINDOW_LANE + NF)
                bias = jnp.where(window & ((gap < -back) | (gap > fwd)), MASKED, bias)
                k_time[frame] = keys
                b_time[frame] = bias.astype(jnp.bfloat16)
                return carry

            lax.fori_loop(0, NF, bias_frame, 0)

            def rows_of(part, carry):
                query = qk_got[slot, 0, pl.ds(part * group, group)].reshape(group_rows, DH)
                frame_lane = WINDOW_LANE + part * group + (group_row >> 6)
                marks = jnp.where((group_lane < 3) | (group_lane == frame_lane), 1.0, 0.0)
                query = jnp.concatenate([query, marks.astype(jnp.bfloat16)], axis=1)
                keys = jnp.concatenate(
                    [k_time[...].reshape(length, DH), b_time[...].reshape(length, DH)], axis=1
                )
                scores = lax.dot_general(query, keys, NT, preferred_element_type=jnp.float32)
                weights, total = softmax_parts(scores)
                probs[slot, part] = weights
                inverse[slot, part] = jnp.broadcast_to(1.0 / total, (group_rows, DH))
                return carry

            lax.fori_loop(0, NF // group, rows_of, 0)

        return carry

    lax.fori_loop(0, SLOTS, weigh, 0)

    def mix(slot, carry):
        exists, row, col = owned(slot, me)

        @pl.when(exists)
        def _():
            got = s_got.at[slot]
            pltpu.make_async_copy(got, got, s_sem.at[slot]).wait()

            def rows_of(part, carry):
                values = s_got[slot].reshape(length, DH)
                mixed = jnp.dot(probs[slot, part], values, preferred_element_type=jnp.float32)
                temporal = (mixed * inverse[slot, part]).astype(jnp.bfloat16).astype(jnp.float32)
                for inside in range(group):
                    frame = part * group + inside
                    valid = token_valid(row, col, rows_ref[frame], cols_ref[frame])
                    both = temporal[inside * AREA : (inside + 1) * AREA] + s_got[slot, frame].astype(
                        jnp.float32
                    )
                    both = jnp.where(valid, both, 0.0).astype(jnp.bfloat16)
                    o_buf[slot, frame] = both.reshape(TS, TS, DH)
                return carry

            lax.fori_loop(0, NF // group, rows_of, 0)

            def give(step, carry):
                frame = peer(NF - step)
                pltpu.make_async_remote_copy(
                    src_ref=o_buf.at[slot, frame], dst_ref=out_ref.at[row, :, col],
                    send_sem=send_sem.at[3], recv_sem=out_sem,
                    device_id={"frame": frame}, device_id_type=MESH,
                ).start()
                return carry

            lax.fori_loop(1, NF, give, 0)
            pltpu.make_async_copy(o_buf.at[slot, me], out_ref.at[row, :, col], out_sem).start()

        return carry

    lax.fori_loop(0, SLOTS, mix, 0)

    pltpu.make_async_copy(out_ref, out_ref, out_sem).wait()
    exists, _, _ = owned(SLOTS - 1, me)

    def drain(owned_count):
        away = s_loc.at[pl.ds(0, tile_rows * tile_cols - owned_count)]
        for part in range(3):
            pltpu.make_async_copy(away, away, send_sem.at[part]).wait()
        sent = s_loc.at[pl.ds(0, owned_count * (NF - 1))]
        pltpu.make_async_copy(sent, sent, send_sem.at[3]).wait()

    @pl.when(exists)
    def _():
        drain(SLOTS)

    @pl.when(jnp.logical_not(exists))
    def _():
        drain(SLOTS - 1)


def per_device(queries, keys, values, back_reach, fwd_reach, valid_rows, valid_cols):
    _, token_rows, token_cols, _ = queries.shape
    tile_rows, tile_cols = token_rows // TS, token_cols // TS
    grid = (tile_rows, TS, tile_cols, TS, DH)
    padded = (tile_rows + 2, tile_cols + 2, AREA, DH)
    bf16 = jnp.bfloat16
    group = 4
    out = pl.pallas_call(
        kernel,
        out_shape=jax.ShapeDtypeStruct(grid, bf16),
        in_specs=[pl.BlockSpec(memory_space=pl.ANY)] * 7,
        out_specs=pl.BlockSpec(memory_space=pl.ANY),
        scratch_shapes=[
            pltpu.SMEM(back_reach.shape, jnp.int32),
            pltpu.SMEM(fwd_reach.shape, jnp.int32),
            pltpu.SMEM(valid_rows.shape, jnp.int32),
            pltpu.SMEM(valid_cols.shape, jnp.int32),
            pltpu.VMEM((tile_rows, tile_cols, TS, TS, DH), bf16),
            pltpu.VMEM((tile_rows, tile_cols, TS, TS, DH), bf16),
            pltpu.VMEM((tile_rows, tile_cols, TS, TS, DH), bf16),
            pltpu.VMEM(padded, bf16),
            pltpu.VMEM(padded, bf16),
            pltpu.VMEM(padded, bf16),
            pltpu.VMEM((tile_rows * tile_cols, AREA, DH), bf16),
            pltpu.VMEM((SLOTS, 2, NF, TS, TS, DH), bf16),
            pltpu.VMEM((SLOTS, NF, AREA, DH), bf16),
            pltpu.VMEM((NF, AREA, DH), bf16),
            pltpu.VMEM((NF, AREA, DH), bf16),
            pltpu.VMEM((SLOTS, NF // group, group * AREA, NF * AREA), bf16),
            pltpu.VMEM((SLOTS, NF // group, group * AREA, DH), jnp.float32),
            pltpu.VMEM((SLOTS, NF, TS, TS, DH), bf16),
            pltpu.SemaphoreType.DMA,
            pltpu.SemaphoreType.DMA((4,)),
            pltpu.SemaphoreType.REGULAR((NF // 2 - 1,)),
            pltpu.SemaphoreType.DMA((4,)),
            pltpu.SemaphoreType.DMA((SLOTS,)),
            pltpu.SemaphoreType.DMA((SLOTS,)),
            pltpu.SemaphoreType.DMA,
        ],
        compiler_params=pltpu.CompilerParams(
            collective_id=0, has_side_effects=True, vmem_limit_bytes=52 << 20
        ),
    )(
        queries.reshape(grid), keys.reshape(grid), values.reshape(grid),
        back_reach, fwd_reach, valid_rows, valid_cols,
    )
    return out.reshape(queries.shape)


def solution(mesh):
    in_specs = (
        P(("dp", "frame"), None, None, "row"),
        P(("dp", "frame"), None, None, "row"),
        P(("dp", "frame"), None, None, "row"),
        P("dp", None),
        P("dp", None),
        P("dp"),
        P("dp"),
    )
    out_specs = P(("dp", "frame"), None, None, "row")
    return jax.shard_map(
        per_device, mesh=mesh, in_specs=in_specs, out_specs=out_specs, check_vma=False
    )
```

```python
import math

import jax
import jax.numpy as jnp
from jax import lax
from jax.experimental import pallas as pl
from jax.experimental.pallas import tpu as pltpu
from jax.sharding import PartitionSpec as P

DH = 128
TS = 8
AREA = TS * TS
NF = 16
SLOTS = 4
WINDOW_LANE = 8
MASKED = -1e30
SCALE = math.log2(math.e) / math.sqrt(DH)
MESH = pl.DeviceIdType.MESH
NT = (((1,), (1,)), ((), ()))


def row_lane(rows):
    return (
        lax.broadcasted_iota(jnp.int32, (rows, DH), 0),
        lax.broadcasted_iota(jnp.int32, (rows, DH), 1),
    )


def token_valid(tile_row, tile_col, rows_ok, cols_ok):
    token, _ = row_lane(AREA)
    return (tile_row * TS + (token >> 3) < rows_ok) & (tile_col * TS + (token & 7) < cols_ok)


def key_bias(keys, valid):
    _, lane = row_lane(AREA)
    wide = keys.astype(jnp.float32)
    half = -0.5 * jnp.sum(wide * wide, axis=1, keepdims=True)
    high = half.astype(jnp.bfloat16).astype(jnp.float32)
    rest = half - high
    middle = rest.astype(jnp.bfloat16).astype(jnp.float32)
    low = rest - middle
    parts = jnp.where(lane == 0, high, jnp.where(lane == 1, middle, jnp.where(lane == 2, low, 0.0)))
    return jnp.where(valid, parts, jnp.where(lane == 0, MASKED, 0.0))


def softmax_parts(scores):
    highest = jnp.max(scores, axis=1, keepdims=True)
    weights = jnp.exp2((scores - highest) * SCALE)
    return weights.astype(jnp.bfloat16), jnp.sum(weights, axis=1, keepdims=True)


def kernel(
    q_hbm, k_hbm, v_hbm, back_hbm, fwd_hbm, rows_hbm, cols_hbm, out_ref,
    back_ref, fwd_ref, rows_ref, cols_ref,
    q_loc, k_loc, v_loc, k_pad, v_pad, b_pad, s_loc, qk_got, s_got, k_time, b_time, probs, inverse, o_buf,
    load_sem, small_sem, stage_sem, send_sem, qk_sem, s_sem, out_sem,
):
    tile_rows, _, tile_cols = q_hbm.shape[:3]
    me = lax.axis_index("frame")
    shift = 2 * lax.rem(lax.axis_index("row"), 2)
    barrier = pltpu.get_barrier_semaphore()

    def peer(step):
        half = (step + 1) // 2
        return lax.rem(me + jnp.where(lax.rem(step, 2) == 1, half, NF - half), NF)

    def owned(slot, owner):
        label = lax.rem(owner + shift, NF)
        last = slot == SLOTS - 1
        exists = jnp.logical_not(last & (lax.rem(label, 4) == 3))
        place = jnp.where(last, label - label // 4, label)
        tile = jnp.minimum(slot * NF + place, tile_rows * tile_cols - 1)
        return exists, tile // tile_cols, lax.rem(tile, tile_cols)

    def announce(semaphore):
        for neighbour in (peer(1), peer(2)):
            pl.semaphore_signal(
                semaphore, inc=1, device_id={"frame": neighbour}, device_id_type=MESH
            )

    announce(barrier)

    small = (
        (back_hbm, back_ref), (fwd_hbm, fwd_ref), (rows_hbm, rows_ref), (cols_hbm, cols_ref)
    )
    for index, (source, target) in enumerate(small):
        pltpu.make_async_copy(source, target, small_sem.at[index]).start()

    def load(col, carry):
        for source, target in ((q_hbm, q_loc), (k_hbm, k_loc), (v_hbm, v_loc)):
            pltpu.make_async_copy(source.at[:, :, col], target.at[:, col], load_sem).start()
        return carry

    lax.fori_loop(0, tile_cols, load, 0)

    def qk_copies(slot, row, col):
        for part, source in ((0, q_hbm), (1, k_hbm)):
            yield part, source.at[row, :, col], qk_got.at[slot, part, me]

    pl.semaphore_wait(barrier, 2)

    def send_qk(distance, carry):
        @pl.when(distance > 1)
        def _():
            announce(stage_sem.at[distance - 2])
            pl.semaphore_wait(stage_sem.at[distance - 2], 2)

        def send(index, carry):
            slot, side = index // 2, lax.rem(index, 2)
            owner = peer(2 * distance - 1 + side)
            exists, row, col = owned(slot, owner)

            @pl.when(exists & jnp.logical_not((distance == NF // 2) & (side == 1)))
            def _():
                for part, source, target in qk_copies(slot, row, col):
                    pltpu.make_async_remote_copy(
                        src_ref=source, dst_ref=target,
                        send_sem=send_sem.at[part], recv_sem=qk_sem.at[slot],
                        device_id={"frame": owner}, device_id_type=MESH,
                    ).start()

            return carry

        return lax.fori_loop(0, 2 * SLOTS, send, carry)

    lax.fori_loop(1, NF // 2 + 1, send_qk, 0)

    def keep_qk(slot, carry):
        exists, row, col = owned(slot, me)

        @pl.when(exists)
        def _():
            for _, source, target in qk_copies(slot, row, col):
                pltpu.make_async_copy(source, target, qk_sem.at[slot]).start()

        return carry

    lax.fori_loop(0, SLOTS, keep_qk, 0)

    nothing = jnp.zeros((AREA, DH), jnp.bfloat16)
    _, lane = row_lane(AREA)
    outside = jnp.where(lane == 0, MASKED, 0.0).astype(jnp.bfloat16)

    def border(row, col):
        k_pad[row, col] = nothing
        v_pad[row, col] = nothing
        b_pad[row, col] = outside

    def border_col(col, carry):
        border(0, col)
        border(tile_rows + 1, col)
        return carry

    def border_row(row, carry):
        border(row, 0)
        border(row, tile_cols + 1)
        return carry

    lax.fori_loop(0, tile_cols + 2, border_col, 0)
    lax.fori_loop(1, tile_rows + 1, border_row, 0)

    for _ in range(3):
        pltpu.make_async_copy(q_loc, q_loc, load_sem).wait()
    for index, (source, target) in enumerate(small):
        pltpu.make_async_copy(source, target, small_sem.at[index]).wait()

    rows_here, cols_here = rows_ref[me], cols_ref[me]

    def bias_tile(tile, carry):
        row, col = tile // tile_cols, lax.rem(tile, tile_cols)
        valid = token_valid(row, col, rows_here, cols_here)
        keys = k_loc[row, col].reshape(AREA, DH)
        k_pad[row + 1, col + 1] = keys
        v_pad[row + 1, col + 1] = v_loc[row, col].reshape(AREA, DH)
        b_pad[row + 1, col + 1] = key_bias(keys, valid).astype(jnp.bfloat16)
        return carry

    lax.fori_loop(0, tile_rows * tile_cols, bias_tile, 0)

    ones = jnp.where(lane < 3, 1.0, 0.0).astype(jnp.bfloat16)

    def near(ref, row, col):
        slabs = [ref[row + dy, pl.ds(col, 3)].reshape(3 * AREA, DH) for dy in range(3)]
        return jnp.concatenate(slabs, axis=0)

    def spatial(index, carry):
        slot, owner = index // NF, peer(lax.rem(index, NF))
        exists, row, col = owned(slot, owner)

        @pl.when(exists)
        def _():
            tile = row * tile_cols + col
            query = jnp.concatenate([q_loc[row, col].reshape(AREA, DH), ones], axis=1)
            keys = jnp.concatenate([near(k_pad, row, col), near(b_pad, row, col)], axis=1)
            scores = lax.dot_general(query, keys, NT, preferred_element_type=jnp.float32)
            weights, total = softmax_parts(scores)
            mixed = jnp.dot(weights, near(v_pad, row, col), preferred_element_type=jnp.float32)
            valid = token_valid(row, col, rows_here, cols_here)
            s_loc[tile] = jnp.where(valid, mixed * (1.0 / total), 0.0).astype(jnp.bfloat16)
            target = s_got.at[slot, me]

            @pl.when(owner != me)
            def _():
                pltpu.make_async_remote_copy(
                    src_ref=s_loc.at[tile], dst_ref=target,
                    send_sem=send_sem.at[2], recv_sem=s_sem.at[slot],
                    device_id={"frame": owner}, device_id_type=MESH,
                ).start()

            @pl.when(owner == me)
            def _():
                pltpu.make_async_copy(s_loc.at[tile], target, s_sem.at[slot]).start()

        return carry

    lax.fori_loop(0, SLOTS * NF, spatial, 0)

    group = 4
    group_rows = group * AREA
    length = NF * AREA
    group_row, group_lane = row_lane(group_rows)

    def weigh(slot, carry):
        exists, row, col = owned(slot, me)

        @pl.when(exists)
        def _():
            got = qk_got.at[slot]
            pltpu.make_async_copy(got, got, qk_sem.at[slot]).wait()
            back, fwd = back_ref[row, col], fwd_ref[row, col]

            def bias_frame(frame, carry):
                valid = token_valid(row, col, rows_ref[frame], cols_ref[frame])
                keys = qk_got[slot, 1, frame].reshape(AREA, DH)
                bias = key_bias(keys, valid)
                gap = frame - (lane - WINDOW_LANE)
                window = (lane >= WINDOW_LANE) & (lane < WINDOW_LANE + NF)
                bias = jnp.where(window & ((gap < -back) | (gap > fwd)), MASKED, bias)
                k_time[frame] = keys
                b_time[frame] = bias.astype(jnp.bfloat16)
                return carry

            lax.fori_loop(0, NF, bias_frame, 0)

            def rows_of(part, carry):
                query = qk_got[slot, 0, pl.ds(part * group, group)].reshape(group_rows, DH)
                frame_lane = WINDOW_LANE + part * group + (group_row >> 6)
                marks = jnp.where((group_lane < 3) | (group_lane == frame_lane), 1.0, 0.0)
                query = jnp.concatenate([query, marks.astype(jnp.bfloat16)], axis=1)
                keys = jnp.concatenate(
                    [k_time[...].reshape(length, DH), b_time[...].reshape(length, DH)], axis=1
                )
                scores = lax.dot_general(query, keys, NT, preferred_element_type=jnp.float32)
                weights, total = softmax_parts(scores)
                probs[slot, part] = weights
                inverse[slot, part] = jnp.broadcast_to(1.0 / total, (group_rows, DH))
                return carry

            lax.fori_loop(0, NF // group, rows_of, 0)

        return carry

    lax.fori_loop(0, SLOTS, weigh, 0)

    def mix(slot, carry):
        exists, row, col = owned(slot, me)

        @pl.when(exists)
        def _():
            got = s_got.at[slot]
            pltpu.make_async_copy(got, got, s_sem.at[slot]).wait()

            def rows_of(part, carry):
                values = s_got[slot].reshape(length, DH)
                mixed = jnp.dot(probs[slot, part], values, preferred_element_type=jnp.float32)
                temporal = (mixed * inverse[slot, part]).astype(jnp.bfloat16).astype(jnp.float32)
                for inside in range(group):
                    frame = part * group + inside
                    valid = token_valid(row, col, rows_ref[frame], cols_ref[frame])
                    both = temporal[inside * AREA : (inside + 1) * AREA] + s_got[slot, frame].astype(
                        jnp.float32
                    )
                    both = jnp.where(valid, both, 0.0).astype(jnp.bfloat16)
                    o_buf[slot, frame] = both.reshape(TS, TS, DH)
                return carry

            lax.fori_loop(0, NF // group, rows_of, 0)

            def give(step, carry):
                frame = peer(NF - step)
                pltpu.make_async_remote_copy(
                    src_ref=o_buf.at[slot, frame], dst_ref=out_ref.at[row, :, col],
                    send_sem=send_sem.at[3], recv_sem=out_sem,
                    device_id={"frame": frame}, device_id_type=MESH,
                ).start()
                return carry

            lax.fori_loop(1, NF, give, 0)
            pltpu.make_async_copy(o_buf.at[slot, me], out_ref.at[row, :, col], out_sem).start()

        return carry

    lax.fori_loop(0, SLOTS, mix, 0)

    pltpu.make_async_copy(out_ref, out_ref, out_sem).wait()
    exists, _, _ = owned(SLOTS - 1, me)

    def drain(owned_count):
        away = s_loc.at[pl.ds(0, tile_rows * tile_cols - owned_count)]
        for part in range(3):
            pltpu.make_async_copy(away, away, send_sem.at[part]).wait()
        sent = s_loc.at[pl.ds(0, owned_count * (NF - 1))]
        pltpu.make_async_copy(sent, sent, send_sem.at[3]).wait()

    @pl.when(exists)
    def _():
        drain(SLOTS)

    @pl.when(jnp.logical_not(exists))
    def _():
        drain(SLOTS - 1)


def per_device(queries, keys, values, back_reach, fwd_reach, valid_rows, valid_cols):
    _, token_rows, token_cols, _ = queries.shape
    tile_rows, tile_cols = token_rows // TS, token_cols // TS
    grid = (tile_rows, TS, tile_cols, TS, DH)
    padded = (tile_rows + 2, tile_cols + 2, AREA, DH)
    bf16 = jnp.bfloat16
    group = 4
    out = pl.pallas_call(
        kernel,
        out_shape=jax.ShapeDtypeStruct(grid, bf16),
        in_specs=[pl.BlockSpec(memory_space=pl.ANY)] * 7,
        out_specs=pl.BlockSpec(memory_space=pl.ANY),
        scratch_shapes=[
            pltpu.SMEM(back_reach.shape, jnp.int32),
            pltpu.SMEM(fwd_reach.shape, jnp.int32),
            pltpu.SMEM(valid_rows.shape, jnp.int32),
            pltpu.SMEM(valid_cols.shape, jnp.int32),
            pltpu.VMEM((tile_rows, tile_cols, TS, TS, DH), bf16),
            pltpu.VMEM((tile_rows, tile_cols, TS, TS, DH), bf16),
            pltpu.VMEM((tile_rows, tile_cols, TS, TS, DH), bf16),
            pltpu.VMEM(padded, bf16),
            pltpu.VMEM(padded, bf16),
            pltpu.VMEM(padded, bf16),
            pltpu.VMEM((tile_rows * tile_cols, AREA, DH), bf16),
            pltpu.VMEM((SLOTS, 2, NF, TS, TS, DH), bf16),
            pltpu.VMEM((SLOTS, NF, AREA, DH), bf16),
            pltpu.VMEM((NF, AREA, DH), bf16),
            pltpu.VMEM((NF, AREA, DH), bf16),
            pltpu.VMEM((SLOTS, NF // group, group * AREA, NF * AREA), bf16),
            pltpu.VMEM((SLOTS, NF // group, group * AREA, DH), jnp.float32),
            pltpu.VMEM((SLOTS, NF, TS, TS, DH), bf16),
            pltpu.SemaphoreType.DMA,
            pltpu.SemaphoreType.DMA((4,)),
            pltpu.SemaphoreType.REGULAR((NF // 2 - 1,)),
            pltpu.SemaphoreType.DMA((4,)),
            pltpu.SemaphoreType.DMA((SLOTS,)),
            pltpu.SemaphoreType.DMA((SLOTS,)),
            pltpu.SemaphoreType.DMA,
        ],
        compiler_params=pltpu.CompilerParams(
            collective_id=0, has_side_effects=True, vmem_limit_bytes=52 << 20
        ),
    )(
        *[
            pltpu.with_memory_space_constraint(array, pltpu.HBM)
            for array in (
                queries.reshape(grid), keys.reshape(grid), values.reshape(grid),
                back_reach, fwd_reach, valid_rows, valid_cols,
            )
        ]
    )
    return out.reshape(queries.shape)


def solution(mesh):
    in_specs = (
        P(("dp", "frame"), None, None, "row"),
        P(("dp", "frame"), None, None, "row"),
        P(("dp", "frame"), None, None, "row"),
        P("dp", None),
        P("dp", None),
        P("dp"),
        P("dp"),
    )
    out_specs = P(("dp", "frame"), None, None, "row")
    return jax.shard_map(
        per_device, mesh=mesh, in_specs=in_specs, out_specs=out_specs, check_vma=False
    )
```

```python
import math

import jax
import jax.numpy as jnp
from jax import lax
from jax.experimental import pallas as pl
from jax.experimental.pallas import tpu as pltpu
from jax.sharding import PartitionSpec as P

DH = 128
TS = 8
AREA = TS * TS
NF = 16
SLOTS = 4
WINDOW_LANE = 8
NEAR = 2
MASKED = -1e30
SCALE = math.log2(math.e) / math.sqrt(DH)
MESH = pl.DeviceIdType.MESH
NT = (((1,), (1,)), ((), ()))


def row_lane(rows):
    return (
        lax.broadcasted_iota(jnp.int32, (rows, DH), 0),
        lax.broadcasted_iota(jnp.int32, (rows, DH), 1),
    )


def token_valid(tile_row, tile_col, rows_ok, cols_ok):
    token, _ = row_lane(AREA)
    return (tile_row * TS + (token >> 3) < rows_ok) & (tile_col * TS + (token & 7) < cols_ok)


def key_bias(keys, valid):
    _, lane = row_lane(AREA)
    wide = keys.astype(jnp.float32)
    half = -0.5 * jnp.sum(wide * wide, axis=1, keepdims=True)
    high = half.astype(jnp.bfloat16).astype(jnp.float32)
    rest = half - high
    middle = rest.astype(jnp.bfloat16).astype(jnp.float32)
    low = rest - middle
    parts = jnp.where(lane == 0, high, jnp.where(lane == 1, middle, jnp.where(lane == 2, low, 0.0)))
    return jnp.where(valid, parts, jnp.where(lane == 0, MASKED, 0.0))


def softmax_parts(scores):
    highest = jnp.max(scores, axis=1, keepdims=True)
    weights = jnp.exp2((scores - highest) * SCALE)
    return weights.astype(jnp.bfloat16), jnp.sum(weights, axis=1, keepdims=True)


def kernel(
    q_hbm, k_hbm, v_hbm, back_hbm, fwd_hbm, rows_hbm, cols_hbm, out_ref,
    back_ref, fwd_ref, rows_ref, cols_ref,
    q_loc, k_loc, v_loc, k_pad, v_pad, b_pad, s_loc, qk_got, s_got, k_time, b_time, probs, inverse, o_buf,
    load_sem, small_sem, stage_sem, send_sem, qk_sem, s_sem, out_sem,
):
    tile_rows, _, tile_cols = q_hbm.shape[:3]
    me = lax.axis_index("frame")
    shift = 2 * lax.rem(lax.axis_index("row"), 2)
    barrier = pltpu.get_barrier_semaphore()

    def peer(step):
        half = (step + 1) // 2
        return lax.rem(me + jnp.where(lax.rem(step, 2) == 1, half, NF - half), NF)

    def owned(slot, owner):
        label = lax.rem(owner + shift, NF)
        last = slot == SLOTS - 1
        exists = jnp.logical_not(last & (lax.rem(label, 4) == 3))
        place = jnp.where(last, label - label // 4, label)
        tile = jnp.minimum(slot * NF + place, tile_rows * tile_cols - 1)
        return exists, tile // tile_cols, lax.rem(tile, tile_cols)

    def announce(semaphore):
        for neighbour in (peer(1), peer(2)):
            pl.semaphore_signal(
                semaphore, inc=1, device_id={"frame": neighbour}, device_id_type=MESH
            )

    announce(barrier)

    small = (
        (back_hbm, back_ref), (fwd_hbm, fwd_ref), (rows_hbm, rows_ref), (cols_hbm, cols_ref)
    )

    def load(col, carry):
        for source, target in ((q_hbm, q_loc), (k_hbm, k_loc), (v_hbm, v_loc)):
            pltpu.make_async_copy(source.at[:, :, col], target.at[:, col], load_sem).start()
        return carry


    def qk_copies(slot, row, col):
        for part, source in ((0, q_hbm), (1, k_hbm)):
            yield part, source.at[row, :, col], qk_got.at[slot, part, me]

    pl.semaphore_wait(barrier, 2)

    def send_qk(distance, carry):
        if not isinstance(distance, int):
            announce(stage_sem.at[distance - 2])
            pl.semaphore_wait(stage_sem.at[distance - 2], 2)

        def send(index, carry):
            slot, side = index // 2, lax.rem(index, 2)
            owner = peer(2 * distance - 1 + side)
            exists, row, col = owned(slot, owner)

            @pl.when(exists & jnp.logical_not((distance == NF // 2) & (side == 1)))
            def _():
                for part, source, target in qk_copies(slot, row, col):
                    pltpu.make_async_remote_copy(
                        src_ref=source, dst_ref=target,
                        send_sem=send_sem.at[part], recv_sem=qk_sem.at[slot],
                        device_id={"frame": owner}, device_id_type=MESH,
                    ).start()

            return carry

        return lax.fori_loop(0, 2 * SLOTS, send, carry)

    send_qk(1, 0)
    for index, (source, target) in enumerate(small):
        pltpu.make_async_copy(source, target, small_sem.at[index]).start()
    lax.fori_loop(0, tile_cols, load, 0)
    lax.fori_loop(2, NF // 2 + 1, send_qk, 0)

    def keep_qk(slot, carry):
        exists, row, col = owned(slot, me)

        @pl.when(exists)
        def _():
            for _, source, target in qk_copies(slot, row, col):
                pltpu.make_async_copy(source, target, qk_sem.at[slot]).start()

        return carry

    lax.fori_loop(0, SLOTS, keep_qk, 0)

    nothing = jnp.zeros((AREA, DH), jnp.bfloat16)
    _, lane = row_lane(AREA)
    outside = jnp.where(lane == 0, MASKED, 0.0).astype(jnp.bfloat16)

    def border(row, col):
        k_pad[row, col] = nothing
        v_pad[row, col] = nothing
        b_pad[row, col] = outside

    def border_col(col, carry):
        border(0, col)
        border(tile_rows + 1, col)
        return carry

    def border_row(row, carry):
        border(row, 0)
        border(row, tile_cols + 1)
        return carry

    lax.fori_loop(0, tile_cols + 2, border_col, 0)
    lax.fori_loop(1, tile_rows + 1, border_row, 0)

    for _ in range(3):
        pltpu.make_async_copy(q_loc, q_loc, load_sem).wait()
    for index, (source, target) in enumerate(small):
        pltpu.make_async_copy(source, target, small_sem.at[index]).wait()

    rows_here, cols_here = rows_ref[me], cols_ref[me]

    def bias_tile(tile, carry):
        row, col = tile // tile_cols, lax.rem(tile, tile_cols)
        valid = token_valid(row, col, rows_here, cols_here)
        keys = k_loc[row, col].reshape(AREA, DH)
        k_pad[row + 1, col + 1] = keys
        v_pad[row + 1, col + 1] = v_loc[row, col].reshape(AREA, DH)
        b_pad[row + 1, col + 1] = key_bias(keys, valid).astype(jnp.bfloat16)
        return carry

    lax.fori_loop(0, tile_rows * tile_cols, bias_tile, 0)

    ones = jnp.where(lane < 3, 1.0, 0.0).astype(jnp.bfloat16)

    def near(ref, row, col):
        slabs = [ref[row + dy, pl.ds(col, 3)].reshape(3 * AREA, DH) for dy in range(3)]
        return jnp.concatenate(slabs, axis=0)

    def spatial(index, carry):
        slot, owner = index // NF, peer(NF - 1 - lax.rem(index, NF))
        exists, row, col = owned(slot, owner)

        @pl.when(exists)
        def _():
            tile = row * tile_cols + col
            query = jnp.concatenate([q_loc[row, col].reshape(AREA, DH), ones], axis=1)
            keys = jnp.concatenate([near(k_pad, row, col), near(b_pad, row, col)], axis=1)
            scores = lax.dot_general(query, keys, NT, preferred_element_type=jnp.float32)
            weights, total = softmax_parts(scores)
            mixed = jnp.dot(weights, near(v_pad, row, col), preferred_element_type=jnp.float32)
            valid = token_valid(row, col, rows_here, cols_here)
            s_loc[tile] = jnp.where(valid, mixed * (1.0 / total), 0.0).astype(jnp.bfloat16)
            target = s_got.at[slot, me]

            @pl.when(owner != me)
            def _():
                pltpu.make_async_remote_copy(
                    src_ref=s_loc.at[tile], dst_ref=target,
                    send_sem=send_sem.at[2], recv_sem=s_sem.at[slot],
                    device_id={"frame": owner}, device_id_type=MESH,
                ).start()

            @pl.when(owner == me)
            def _():
                pltpu.make_async_copy(s_loc.at[tile], target, s_sem.at[slot]).start()

        return carry

    lax.fori_loop(0, SLOTS * NF, spatial, 0)

    group = 4
    group_rows = group * AREA
    length = NF * AREA
    group_row, group_lane = row_lane(group_rows)

    def weigh(slot, carry):
        exists, row, col = owned(slot, me)

        @pl.when(exists)
        def _():
            got = qk_got.at[slot]
            pltpu.make_async_copy(got, got, qk_sem.at[slot]).wait()
            back, fwd = back_ref[row, col], fwd_ref[row, col]

            def bias_frame(frame, carry):
                valid = token_valid(row, col, rows_ref[frame], cols_ref[frame])
                keys = qk_got[slot, 1, frame].reshape(AREA, DH)
                bias = key_bias(keys, valid)
                gap = frame - (lane - WINDOW_LANE)
                window = (lane >= WINDOW_LANE) & (lane < WINDOW_LANE + NF)
                bias = jnp.where(window & ((gap < -back) | (gap > fwd)), MASKED, bias)
                k_time[frame] = keys
                b_time[frame] = bias.astype(jnp.bfloat16)
                return carry

            lax.fori_loop(0, NF, bias_frame, 0)

            def rows_of(part, carry):
                query = qk_got[slot, 0, pl.ds(part * group, group)].reshape(group_rows, DH)
                frame_lane = WINDOW_LANE + part * group + (group_row >> 6)
                marks = jnp.where((group_lane < 3) | (group_lane == frame_lane), 1.0, 0.0)
                query = jnp.concatenate([query, marks.astype(jnp.bfloat16)], axis=1)
                keys = jnp.concatenate(
                    [k_time[...].reshape(length, DH), b_time[...].reshape(length, DH)], axis=1
                )
                scores = lax.dot_general(query, keys, NT, preferred_element_type=jnp.float32)
                weights, total = softmax_parts(scores)
                probs[slot, part] = weights
                inverse[slot, part] = jnp.broadcast_to(1.0 / total, (group_rows, DH))
                return carry

            lax.fori_loop(0, NF // group, rows_of, 0)

        return carry

    lax.fori_loop(0, SLOTS, weigh, 0)

    def give(slot, row, col, first, end):
        def one(index, carry):
            frame = peer(end - 1 - index)
            pltpu.make_async_remote_copy(
                src_ref=o_buf.at[slot, frame], dst_ref=out_ref.at[row, :, col],
                send_sem=send_sem.at[3], recv_sem=out_sem,
                device_id={"frame": frame}, device_id_type=MESH,
            ).start()
            return carry

        lax.fori_loop(0, end - first, one, 0)

    def mix(slot, carry):
        exists, row, col = owned(slot, me)

        @pl.when(exists)
        def _():
            got = s_got.at[slot]
            pltpu.make_async_copy(got, got, s_sem.at[slot]).wait()

            def rows_of(part, carry):
                values = s_got[slot].reshape(length, DH)
                mixed = jnp.dot(probs[slot, part], values, preferred_element_type=jnp.float32)
                temporal = (mixed * inverse[slot, part]).astype(jnp.bfloat16).astype(jnp.float32)
                for inside in range(group):
                    frame = part * group + inside
                    valid = token_valid(row, col, rows_ref[frame], cols_ref[frame])
                    both = temporal[inside * AREA : (inside + 1) * AREA] + s_got[slot, frame].astype(
                        jnp.float32
                    )
                    both = jnp.where(valid, both, 0.0).astype(jnp.bfloat16)
                    o_buf[slot, frame] = both.reshape(TS, TS, DH)
                return carry

            lax.fori_loop(0, NF // group, rows_of, 0)

            give(slot, row, col, NEAR + 1, NF)
            pltpu.make_async_copy(o_buf.at[slot, me], out_ref.at[row, :, col], out_sem).start()

        return carry

    lax.fori_loop(0, SLOTS, mix, 0)

    def give_near(slot, carry):
        exists, row, col = owned(slot, me)

        @pl.when(exists)
        def _():
            give(slot, row, col, 1, NEAR + 1)

        return carry

    lax.fori_loop(0, SLOTS, give_near, 0)

    pltpu.make_async_copy(out_ref, out_ref, out_sem).wait()
    exists, _, _ = owned(SLOTS - 1, me)

    def drain(owned_count):
        away = s_loc.at[pl.ds(0, tile_rows * tile_cols - owned_count)]
        for part in range(3):
            pltpu.make_async_copy(away, away, send_sem.at[part]).wait()
        sent = s_loc.at[pl.ds(0, owned_count * (NF - 1))]
        pltpu.make_async_copy(sent, sent, send_sem.at[3]).wait()

    @pl.when(exists)
    def _():
        drain(SLOTS)

    @pl.when(jnp.logical_not(exists))
    def _():
        drain(SLOTS - 1)


def per_device(queries, keys, values, back_reach, fwd_reach, valid_rows, valid_cols):
    _, token_rows, token_cols, _ = queries.shape
    tile_rows, tile_cols = token_rows // TS, token_cols // TS
    grid = (tile_rows, TS, tile_cols, TS, DH)
    padded = (tile_rows + 2, tile_cols + 2, AREA, DH)
    bf16 = jnp.bfloat16
    group = 4
    out = pl.pallas_call(
        kernel,
        out_shape=jax.ShapeDtypeStruct(grid, bf16),
        in_specs=[pl.BlockSpec(memory_space=pl.ANY)] * 7,
        out_specs=pl.BlockSpec(memory_space=pl.ANY),
        scratch_shapes=[
            pltpu.SMEM(back_reach.shape, jnp.int32),
            pltpu.SMEM(fwd_reach.shape, jnp.int32),
            pltpu.SMEM(valid_rows.shape, jnp.int32),
            pltpu.SMEM(valid_cols.shape, jnp.int32),
            pltpu.VMEM((tile_rows, tile_cols, TS, TS, DH), bf16),
            pltpu.VMEM((tile_rows, tile_cols, TS, TS, DH), bf16),
            pltpu.VMEM((tile_rows, tile_cols, TS, TS, DH), bf16),
            pltpu.VMEM(padded, bf16),
            pltpu.VMEM(padded, bf16),
            pltpu.VMEM(padded, bf16),
            pltpu.VMEM((tile_rows * tile_cols, AREA, DH), bf16),
            pltpu.VMEM((SLOTS, 2, NF, TS, TS, DH), bf16),
            pltpu.VMEM((SLOTS, NF, AREA, DH), bf16),
            pltpu.VMEM((NF, AREA, DH), bf16),
            pltpu.VMEM((NF, AREA, DH), bf16),
            pltpu.VMEM((SLOTS, NF // group, group * AREA, NF * AREA), bf16),
            pltpu.VMEM((SLOTS, NF // group, group * AREA, DH), jnp.float32),
            pltpu.VMEM((SLOTS, NF, TS, TS, DH), bf16),
            pltpu.SemaphoreType.DMA,
            pltpu.SemaphoreType.DMA((4,)),
            pltpu.SemaphoreType.REGULAR((NF // 2 - 1,)),
            pltpu.SemaphoreType.DMA((4,)),
            pltpu.SemaphoreType.DMA((SLOTS,)),
            pltpu.SemaphoreType.DMA((SLOTS,)),
            pltpu.SemaphoreType.DMA,
        ],
        compiler_params=pltpu.CompilerParams(
            collective_id=0, has_side_effects=True, vmem_limit_bytes=52 << 20
        ),
    )(
        *[
            pltpu.with_memory_space_constraint(array, pltpu.HBM)
            for array in (
                queries.reshape(grid), keys.reshape(grid), values.reshape(grid),
                back_reach, fwd_reach, valid_rows, valid_cols,
            )
        ]
    )
    return out.reshape(queries.shape)


def solution(mesh):
    in_specs = (
        P(("dp", "frame"), None, None, "row"),
        P(("dp", "frame"), None, None, "row"),
        P(("dp", "frame"), None, None, "row"),
        P("dp", None),
        P("dp", None),
        P("dp"),
        P("dp"),
    )
    out_specs = P(("dp", "frame"), None, None, "row")
    return jax.shard_map(
        per_device, mesh=mesh, in_specs=in_specs, out_specs=out_specs, check_vma=False
    )
```

```python
import math

import jax
import jax.numpy as jnp
from jax import lax
from jax.experimental import pallas as pl
from jax.experimental.pallas import tpu as pltpu
from jax.sharding import PartitionSpec as P

DH = 128
TS = 8
AREA = TS * TS
NF = 16
SLOTS = 4
WINDOW_LANE = 8
NEAR = 2
MASKED = -1e30
SCALE = math.log2(math.e) / math.sqrt(DH)
MESH = pl.DeviceIdType.MESH
NT = (((1,), (1,)), ((), ()))


def row_lane(rows):
    return (
        lax.broadcasted_iota(jnp.int32, (rows, DH), 0),
        lax.broadcasted_iota(jnp.int32, (rows, DH), 1),
    )


def token_valid(tile_row, tile_col, rows_ok, cols_ok):
    token, _ = row_lane(AREA)
    return (tile_row * TS + (token >> 3) < rows_ok) & (tile_col * TS + (token & 7) < cols_ok)


def key_bias(keys, valid):
    _, lane = row_lane(AREA)
    wide = keys.astype(jnp.float32)
    half = -0.5 * jnp.sum(wide * wide, axis=1, keepdims=True)
    high = half.astype(jnp.bfloat16).astype(jnp.float32)
    rest = half - high
    middle = rest.astype(jnp.bfloat16).astype(jnp.float32)
    low = rest - middle
    parts = jnp.where(lane == 0, high, jnp.where(lane == 1, middle, jnp.where(lane == 2, low, 0.0)))
    return jnp.where(valid, parts, jnp.where(lane == 0, MASKED, 0.0))


def softmax_parts(scores):
    highest = jnp.max(scores, axis=1, keepdims=True)
    weights = jnp.exp2((scores - highest) * SCALE)
    return weights.astype(jnp.bfloat16), jnp.sum(weights, axis=1, keepdims=True)


def kernel(
    q_hbm, k_hbm, v_hbm, back_hbm, fwd_hbm, rows_hbm, cols_hbm, out_ref,
    back_ref, fwd_ref, rows_ref, cols_ref,
    q_loc, k_loc, v_loc, k_pad, v_pad, b_pad, s_loc, qk_got, s_got, k_time, b_time, probs, inverse, o_buf,
    load_sem, small_sem, stage_sem, send_sem, qk_sem, s_sem, out_sem,
):
    tile_rows, _, tile_cols = q_hbm.shape[:3]
    me = lax.axis_index("frame")
    shift = 2 * lax.rem(lax.axis_index("row"), 2)
    barrier = pltpu.get_barrier_semaphore()

    def peer(step):
        half = (step + 1) // 2
        return lax.rem(me + jnp.where(lax.rem(step, 2) == 1, half, NF - half), NF)

    def owned(slot, owner):
        label = lax.rem(owner + shift, NF)
        last = slot == SLOTS - 1
        exists = jnp.logical_not(last & (lax.rem(label, 4) == 3))
        place = jnp.where(last, label - label // 4, label)
        tile = jnp.minimum(slot * NF + place, tile_rows * tile_cols - 1)
        return exists, tile // tile_cols, lax.rem(tile, tile_cols)

    def announce(semaphore):
        for neighbour in (peer(1), peer(2)):
            pl.semaphore_signal(
                semaphore, inc=1, device_id={"frame": neighbour}, device_id_type=MESH
            )

    announce(barrier)

    small = (
        (back_hbm, back_ref), (fwd_hbm, fwd_ref), (rows_hbm, rows_ref), (cols_hbm, cols_ref)
    )

    def load(col, carry):
        for source, target in ((q_hbm, q_loc), (k_hbm, k_loc), (v_hbm, v_loc)):
            pltpu.make_async_copy(source.at[:, :, col], target.at[:, col], load_sem).start()
        return carry


    def qk_copies(slot, row, col):
        for part, source in ((0, q_hbm), (1, k_hbm)):
            yield part, source.at[row, :, col], qk_got.at[slot, part, me]

    pl.semaphore_wait(barrier, 2)

    def send_qk(distance, carry):
        if not isinstance(distance, int):
            pl.semaphore_wait(stage_sem.at[distance - 2], 2)

        @pl.when(distance < NF // 2)
        def _():
            announce(stage_sem.at[distance - 1])

        def send(index, carry):
            slot, side = index // 2, lax.rem(index, 2)
            owner = peer(2 * distance - 1 + side)
            exists, row, col = owned(slot, owner)

            @pl.when(exists & jnp.logical_not((distance == NF // 2) & (side == 1)))
            def _():
                for part, source, target in qk_copies(slot, row, col):
                    pltpu.make_async_remote_copy(
                        src_ref=source, dst_ref=target,
                        send_sem=send_sem.at[part], recv_sem=qk_sem.at[slot],
                        device_id={"frame": owner}, device_id_type=MESH,
                    ).start()

            return carry

        return lax.fori_loop(0, 2 * SLOTS, send, carry)

    send_qk(1, 0)
    for index, (source, target) in enumerate(small):
        pltpu.make_async_copy(source, target, small_sem.at[index]).start()
    lax.fori_loop(0, tile_cols, load, 0)
    lax.fori_loop(2, NF // 2 + 1, send_qk, 0)

    def keep_qk(slot, carry):
        exists, row, col = owned(slot, me)

        @pl.when(exists)
        def _():
            for _, source, target in qk_copies(slot, row, col):
                pltpu.make_async_copy(source, target, qk_sem.at[slot]).start()

        return carry

    lax.fori_loop(0, SLOTS, keep_qk, 0)

    nothing = jnp.zeros((AREA, DH), jnp.bfloat16)
    _, lane = row_lane(AREA)
    outside = jnp.where(lane == 0, MASKED, 0.0).astype(jnp.bfloat16)

    def border(row, col):
        k_pad[row, col] = nothing
        v_pad[row, col] = nothing
        b_pad[row, col] = outside

    def border_col(col, carry):
        border(0, col)
        border(tile_rows + 1, col)
        return carry

    def border_row(row, carry):
        border(row, 0)
        border(row, tile_cols + 1)
        return carry

    lax.fori_loop(0, tile_cols + 2, border_col, 0)
    lax.fori_loop(1, tile_rows + 1, border_row, 0)

    for _ in range(3):
        pltpu.make_async_copy(q_loc, q_loc, load_sem).wait()
    for index, (source, target) in enumerate(small):
        pltpu.make_async_copy(source, target, small_sem.at[index]).wait()

    rows_here, cols_here = rows_ref[me], cols_ref[me]

    def bias_tile(tile, carry):
        row, col = tile // tile_cols, lax.rem(tile, tile_cols)
        valid = token_valid(row, col, rows_here, cols_here)
        keys = k_loc[row, col].reshape(AREA, DH)
        k_pad[row + 1, col + 1] = keys
        v_pad[row + 1, col + 1] = v_loc[row, col].reshape(AREA, DH)
        b_pad[row + 1, col + 1] = key_bias(keys, valid).astype(jnp.bfloat16)
        return carry

    lax.fori_loop(0, tile_rows * tile_cols, bias_tile, 0)

    ones = jnp.where(lane < 3, 1.0, 0.0).astype(jnp.bfloat16)

    def near(ref, row, col):
        slabs = [ref[row + dy, pl.ds(col, 3)].reshape(3 * AREA, DH) for dy in range(3)]
        return jnp.concatenate(slabs, axis=0)

    def spatial(index, carry):
        slot, owner = index // NF, peer(NF - 1 - lax.rem(index, NF))
        exists, row, col = owned(slot, owner)

        @pl.when(exists)
        def _():
            tile = row * tile_cols + col
            query = jnp.concatenate([q_loc[row, col].reshape(AREA, DH), ones], axis=1)
            keys = jnp.concatenate([near(k_pad, row, col), near(b_pad, row, col)], axis=1)
            scores = lax.dot_general(query, keys, NT, preferred_element_type=jnp.float32)
            weights, total = softmax_parts(scores)
            mixed = jnp.dot(weights, near(v_pad, row, col), preferred_element_type=jnp.float32)
            valid = token_valid(row, col, rows_here, cols_here)
            s_loc[tile] = jnp.where(valid, mixed * (1.0 / total), 0.0).astype(jnp.bfloat16)
            target = s_got.at[slot, me]

            @pl.when(owner != me)
            def _():
                pltpu.make_async_remote_copy(
                    src_ref=s_loc.at[tile], dst_ref=target,
                    send_sem=send_sem.at[2], recv_sem=s_sem.at[slot],
                    device_id={"frame": owner}, device_id_type=MESH,
                ).start()

            @pl.when(owner == me)
            def _():
                pltpu.make_async_copy(s_loc.at[tile], target, s_sem.at[slot]).start()

        return carry

    lax.fori_loop(0, SLOTS * NF, spatial, 0)

    group = 4
    group_rows = group * AREA
    length = NF * AREA
    group_row, group_lane = row_lane(group_rows)

    def weigh(slot, carry):
        exists, row, col = owned(slot, me)

        @pl.when(exists)
        def _():
            got = qk_got.at[slot]
            pltpu.make_async_copy(got, got, qk_sem.at[slot]).wait()
            back, fwd = back_ref[row, col], fwd_ref[row, col]

            def bias_frame(frame, carry):
                valid = token_valid(row, col, rows_ref[frame], cols_ref[frame])
                keys = qk_got[slot, 1, frame].reshape(AREA, DH)
                bias = key_bias(keys, valid)
                gap = frame - (lane - WINDOW_LANE)
                window = (lane >= WINDOW_LANE) & (lane < WINDOW_LANE + NF)
                bias = jnp.where(window & ((gap < -back) | (gap > fwd)), MASKED, bias)
                k_time[frame] = keys
                b_time[frame] = bias.astype(jnp.bfloat16)
                return carry

            lax.fori_loop(0, NF, bias_frame, 0)

            def rows_of(part, carry):
                query = qk_got[slot, 0, pl.ds(part * group, group)].reshape(group_rows, DH)
                frame_lane = WINDOW_LANE + part * group + (group_row >> 6)
                marks = jnp.where((group_lane < 3) | (group_lane == frame_lane), 1.0, 0.0)
                query = jnp.concatenate([query, marks.astype(jnp.bfloat16)], axis=1)
                keys = jnp.concatenate(
                    [k_time[...].reshape(length, DH), b_time[...].reshape(length, DH)], axis=1
                )
                scores = lax.dot_general(query, keys, NT, preferred_element_type=jnp.float32)
                weights, total = softmax_parts(scores)
                probs[slot, part] = weights
                inverse[slot, part] = jnp.broadcast_to(1.0 / total, (group_rows, DH))
                return carry

            lax.fori_loop(0, NF // group, rows_of, 0)

        return carry

    lax.fori_loop(0, SLOTS, weigh, 0)

    def give(slot, row, col, first, end):
        def one(index, carry):
            frame = peer(end - 1 - index)
            pltpu.make_async_remote_copy(
                src_ref=o_buf.at[slot, frame], dst_ref=out_ref.at[row, :, col],
                send_sem=send_sem.at[3], recv_sem=out_sem,
                device_id={"frame": frame}, device_id_type=MESH,
            ).start()
            return carry

        lax.fori_loop(0, end - first, one, 0)

    def mix(slot, carry):
        exists, row, col = owned(slot, me)

        @pl.when(exists)
        def _():
            got = s_got.at[slot]
            pltpu.make_async_copy(got, got, s_sem.at[slot]).wait()

            def rows_of(part, carry):
                values = s_got[slot].reshape(length, DH)
                mixed = jnp.dot(probs[slot, part], values, preferred_element_type=jnp.float32)
                temporal = (mixed * inverse[slot, part]).astype(jnp.bfloat16).astype(jnp.float32)
                for inside in range(group):
                    frame = part * group + inside
                    valid = token_valid(row, col, rows_ref[frame], cols_ref[frame])
                    both = temporal[inside * AREA : (inside + 1) * AREA] + s_got[slot, frame].astype(
                        jnp.float32
                    )
                    both = jnp.where(valid, both, 0.0).astype(jnp.bfloat16)
                    o_buf[slot, frame] = both.reshape(TS, TS, DH)
                return carry

            lax.fori_loop(0, NF // group, rows_of, 0)

            give(slot, row, col, NEAR + 1, NF)
            pltpu.make_async_copy(o_buf.at[slot, me], out_ref.at[row, :, col], out_sem).start()

        return carry

    lax.fori_loop(0, SLOTS, mix, 0)

    def give_near(slot, carry):
        exists, row, col = owned(slot, me)

        @pl.when(exists)
        def _():
            give(slot, row, col, 1, NEAR + 1)

        return carry

    lax.fori_loop(0, SLOTS, give_near, 0)

    pltpu.make_async_copy(out_ref, out_ref, out_sem).wait()
    exists, _, _ = owned(SLOTS - 1, me)

    def drain(owned_count):
        away = s_loc.at[pl.ds(0, tile_rows * tile_cols - owned_count)]
        for part in range(3):
            pltpu.make_async_copy(away, away, send_sem.at[part]).wait()
        sent = s_loc.at[pl.ds(0, owned_count * (NF - 1))]
        pltpu.make_async_copy(sent, sent, send_sem.at[3]).wait()

    @pl.when(exists)
    def _():
        drain(SLOTS)

    @pl.when(jnp.logical_not(exists))
    def _():
        drain(SLOTS - 1)


def per_device(queries, keys, values, back_reach, fwd_reach, valid_rows, valid_cols):
    _, token_rows, token_cols, _ = queries.shape
    tile_rows, tile_cols = token_rows // TS, token_cols // TS
    grid = (tile_rows, TS, tile_cols, TS, DH)
    padded = (tile_rows + 2, tile_cols + 2, AREA, DH)
    bf16 = jnp.bfloat16
    group = 4
    out = pl.pallas_call(
        kernel,
        out_shape=jax.ShapeDtypeStruct(grid, bf16),
        in_specs=[pl.BlockSpec(memory_space=pl.ANY)] * 7,
        out_specs=pl.BlockSpec(memory_space=pl.ANY),
        scratch_shapes=[
            pltpu.SMEM(back_reach.shape, jnp.int32),
            pltpu.SMEM(fwd_reach.shape, jnp.int32),
            pltpu.SMEM(valid_rows.shape, jnp.int32),
            pltpu.SMEM(valid_cols.shape, jnp.int32),
            pltpu.VMEM((tile_rows, tile_cols, TS, TS, DH), bf16),
            pltpu.VMEM((tile_rows, tile_cols, TS, TS, DH), bf16),
            pltpu.VMEM((tile_rows, tile_cols, TS, TS, DH), bf16),
            pltpu.VMEM(padded, bf16),
            pltpu.VMEM(padded, bf16),
            pltpu.VMEM(padded, bf16),
            pltpu.VMEM((tile_rows * tile_cols, AREA, DH), bf16),
            pltpu.VMEM((SLOTS, 2, NF, TS, TS, DH), bf16),
            pltpu.VMEM((SLOTS, NF, AREA, DH), bf16),
            pltpu.VMEM((NF, AREA, DH), bf16),
            pltpu.VMEM((NF, AREA, DH), bf16),
            pltpu.VMEM((SLOTS, NF // group, group * AREA, NF * AREA), bf16),
            pltpu.VMEM((SLOTS, NF // group, group * AREA, DH), jnp.float32),
            pltpu.VMEM((SLOTS, NF, TS, TS, DH), bf16),
            pltpu.SemaphoreType.DMA,
            pltpu.SemaphoreType.DMA((4,)),
            pltpu.SemaphoreType.REGULAR((NF // 2 - 1,)),
            pltpu.SemaphoreType.DMA((4,)),
            pltpu.SemaphoreType.DMA((SLOTS,)),
            pltpu.SemaphoreType.DMA((SLOTS,)),
            pltpu.SemaphoreType.DMA,
        ],
        compiler_params=pltpu.CompilerParams(
            collective_id=0, has_side_effects=True, vmem_limit_bytes=52 << 20
        ),
    )(
        *[
            pltpu.with_memory_space_constraint(array, pltpu.HBM)
            for array in (
                queries.reshape(grid), keys.reshape(grid), values.reshape(grid),
                back_reach, fwd_reach, valid_rows, valid_cols,
            )
        ]
    )
    return out.reshape(queries.shape)


def solution(mesh):
    in_specs = (
        P(("dp", "frame"), None, None, "row"),
        P(("dp", "frame"), None, None, "row"),
        P(("dp", "frame"), None, None, "row"),
        P("dp", None),
        P("dp", None),
        P("dp"),
        P("dp"),
    )
    out_specs = P(("dp", "frame"), None, None, "row")
    return jax.shard_map(
        per_device, mesh=mesh, in_specs=in_specs, out_specs=out_specs, check_vma=False
    )
```

```python
import math

import jax
import jax.numpy as jnp
from jax import lax
from jax.experimental import pallas as pl
from jax.experimental.pallas import tpu as pltpu
from jax.sharding import PartitionSpec as P

DH = 128
TS = 8
AREA = TS * TS
NF = 16
SLOTS = 4
WINDOW_LANE = 8
STAGES = 4
NEAR = 2
MASKED = -1e30
SCALE = math.log2(math.e) / math.sqrt(DH)
MESH = pl.DeviceIdType.MESH
NT = (((1,), (1,)), ((), ()))


def row_lane(rows):
    return (
        lax.broadcasted_iota(jnp.int32, (rows, DH), 0),
        lax.broadcasted_iota(jnp.int32, (rows, DH), 1),
    )


def token_valid(tile_row, tile_col, rows_ok, cols_ok):
    token, _ = row_lane(AREA)
    return (tile_row * TS + (token >> 3) < rows_ok) & (tile_col * TS + (token & 7) < cols_ok)


def key_bias(keys, valid):
    _, lane = row_lane(AREA)
    wide = keys.astype(jnp.float32)
    half = -0.5 * jnp.sum(wide * wide, axis=1, keepdims=True)
    high = half.astype(jnp.bfloat16).astype(jnp.float32)
    rest = half - high
    middle = rest.astype(jnp.bfloat16).astype(jnp.float32)
    low = rest - middle
    parts = jnp.where(lane == 0, high, jnp.where(lane == 1, middle, jnp.where(lane == 2, low, 0.0)))
    return jnp.where(valid, parts, jnp.where(lane == 0, MASKED, 0.0))


def softmax_parts(scores):
    highest = jnp.max(scores, axis=1, keepdims=True)
    weights = jnp.exp2((scores - highest) * SCALE)
    return weights.astype(jnp.bfloat16), jnp.sum(weights, axis=1, keepdims=True)


def kernel(
    q_hbm, k_hbm, v_hbm, back_hbm, fwd_hbm, rows_hbm, cols_hbm, out_ref,
    back_ref, fwd_ref, rows_ref, cols_ref,
    q_loc, k_loc, v_loc, k_pad, v_pad, b_pad, s_loc, qk_got, s_got, k_time, b_time, probs, inverse, o_buf,
    load_sem, small_sem, stage_sem, send_sem, qk_sem, s_sem, out_sem,
):
    tile_rows, _, tile_cols = q_hbm.shape[:3]
    me = lax.axis_index("frame")
    shift = 2 * lax.rem(lax.axis_index("row"), 2)
    barrier = pltpu.get_barrier_semaphore()

    def peer(step):
        half = (step + 1) // 2
        return lax.rem(me + jnp.where(lax.rem(step, 2) == 1, half, NF - half), NF)

    def owned(slot, owner):
        label = lax.rem(owner + shift, NF)
        last = slot == SLOTS - 1
        exists = jnp.logical_not(last & (lax.rem(label, 4) == 3))
        place = jnp.where(last, label - label // 4, label)
        tile = jnp.minimum(slot * NF + place, tile_rows * tile_cols - 1)
        return exists, tile // tile_cols, lax.rem(tile, tile_cols)

    def announce(semaphore, hops):
        for neighbour in (peer(2 * hops - 1), peer(2 * hops)):
            pl.semaphore_signal(
                semaphore, inc=1, device_id={"frame": neighbour}, device_id_type=MESH
            )

    announce(barrier, 1)

    small = (
        (back_hbm, back_ref), (fwd_hbm, fwd_ref), (rows_hbm, rows_ref), (cols_hbm, cols_ref)
    )

    def load(col, carry):
        for source, target in ((q_hbm, q_loc), (k_hbm, k_loc), (v_hbm, v_loc)):
            pltpu.make_async_copy(source.at[:, :, col], target.at[:, col], load_sem).start()
        return carry


    def qk_copies(slot, row, col):
        for part, source in ((0, q_hbm), (1, k_hbm)):
            yield part, source.at[row, :, col], qk_got.at[slot, part, me]

    pl.semaphore_wait(barrier, 2)

    def send_qk(distance, carry):

        def send(index, carry):
            slot, side = index // 2, lax.rem(index, 2)
            owner = peer(2 * distance - 1 + side)
            exists, row, col = owned(slot, owner)

            @pl.when(exists & jnp.logical_not((distance == NF // 2) & (side == 1)))
            def _():
                for part, source, target in qk_copies(slot, row, col):
                    pltpu.make_async_remote_copy(
                        src_ref=source, dst_ref=target,
                        send_sem=send_sem.at[part], recv_sem=qk_sem.at[slot],
                        device_id={"frame": owner}, device_id_type=MESH,
                    ).start()

            return carry

        return lax.fori_loop(0, 2 * SLOTS, send, carry)

    reach = 1
    for stage in range(STAGES):
        if stage > 0:
            pl.semaphore_wait(stage_sem.at[stage - 1], 2)
        if stage < STAGES - 1:
            announce(stage_sem.at[stage], reach)
        lax.fori_loop(reach // 2 + 1, reach + 1, send_qk, 0)
        reach *= 2

    for index, (source, target) in enumerate(small):
        pltpu.make_async_copy(source, target, small_sem.at[index]).start()
    lax.fori_loop(0, tile_cols, load, 0)

    def keep_qk(slot, carry):
        exists, row, col = owned(slot, me)

        @pl.when(exists)
        def _():
            for _, source, target in qk_copies(slot, row, col):
                pltpu.make_async_copy(source, target, qk_sem.at[slot]).start()

        return carry

    lax.fori_loop(0, SLOTS, keep_qk, 0)

    nothing = jnp.zeros((AREA, DH), jnp.bfloat16)
    _, lane = row_lane(AREA)
    outside = jnp.where(lane == 0, MASKED, 0.0).astype(jnp.bfloat16)

    def border(row, col):
        k_pad[row, col] = nothing
        v_pad[row, col] = nothing
        b_pad[row, col] = outside

    def border_col(col, carry):
        border(0, col)
        border(tile_rows + 1, col)
        return carry

    def border_row(row, carry):
        border(row, 0)
        border(row, tile_cols + 1)
        return carry

    lax.fori_loop(0, tile_cols + 2, border_col, 0)
    lax.fori_loop(1, tile_rows + 1, border_row, 0)

    for _ in range(3):
        pltpu.make_async_copy(q_loc, q_loc, load_sem).wait()
    for index, (source, target) in enumerate(small):
        pltpu.make_async_copy(source, target, small_sem.at[index]).wait()

    rows_here, cols_here = rows_ref[me], cols_ref[me]

    def bias_tile(tile, carry):
        row, col = tile // tile_cols, lax.rem(tile, tile_cols)
        valid = token_valid(row, col, rows_here, cols_here)
        keys = k_loc[row, col].reshape(AREA, DH)
        k_pad[row + 1, col + 1] = keys
        v_pad[row + 1, col + 1] = v_loc[row, col].reshape(AREA, DH)
        b_pad[row + 1, col + 1] = key_bias(keys, valid).astype(jnp.bfloat16)
        return carry

    lax.fori_loop(0, tile_rows * tile_cols, bias_tile, 0)

    ones = jnp.where(lane < 3, 1.0, 0.0).astype(jnp.bfloat16)

    def near(ref, row, col):
        slabs = [ref[row + dy, pl.ds(col, 3)].reshape(3 * AREA, DH) for dy in range(3)]
        return jnp.concatenate(slabs, axis=0)

    def spatial(index, carry):
        slot, owner = index // NF, peer(NF - 1 - lax.rem(index, NF))
        exists, row, col = owned(slot, owner)

        @pl.when(exists)
        def _():
            tile = row * tile_cols + col
            query = jnp.concatenate([q_loc[row, col].reshape(AREA, DH), ones], axis=1)
            keys = jnp.concatenate([near(k_pad, row, col), near(b_pad, row, col)], axis=1)
            scores = lax.dot_general(query, keys, NT, preferred_element_type=jnp.float32)
            weights, total = softmax_parts(scores)
            mixed = jnp.dot(weights, near(v_pad, row, col), preferred_element_type=jnp.float32)
            valid = token_valid(row, col, rows_here, cols_here)
            s_loc[tile] = jnp.where(valid, mixed * (1.0 / total), 0.0).astype(jnp.bfloat16)
            target = s_got.at[slot, me]

            @pl.when(owner != me)
            def _():
                pltpu.make_async_remote_copy(
                    src_ref=s_loc.at[tile], dst_ref=target,
                    send_sem=send_sem.at[2], recv_sem=s_sem.at[slot],
                    device_id={"frame": owner}, device_id_type=MESH,
                ).start()

            @pl.when(owner == me)
            def _():
                pltpu.make_async_copy(s_loc.at[tile], target, s_sem.at[slot]).start()

        return carry

    lax.fori_loop(0, SLOTS * NF, spatial, 0)

    group = 4
    group_rows = group * AREA
    length = NF * AREA
    group_row, group_lane = row_lane(group_rows)

    def weigh(slot, carry):
        exists, row, col = owned(slot, me)

        @pl.when(exists)
        def _():
            got = qk_got.at[slot]
            pltpu.make_async_copy(got, got, qk_sem.at[slot]).wait()
            back, fwd = back_ref[row, col], fwd_ref[row, col]

            def bias_frame(frame, carry):
                valid = token_valid(row, col, rows_ref[frame], cols_ref[frame])
                keys = qk_got[slot, 1, frame].reshape(AREA, DH)
                bias = key_bias(keys, valid)
                gap = frame - (lane - WINDOW_LANE)
                window = (lane >= WINDOW_LANE) & (lane < WINDOW_LANE + NF)
                bias = jnp.where(window & ((gap < -back) | (gap > fwd)), MASKED, bias)
                k_time[frame] = keys
                b_time[frame] = bias.astype(jnp.bfloat16)
                return carry

            lax.fori_loop(0, NF, bias_frame, 0)

            def rows_of(part, carry):
                query = qk_got[slot, 0, pl.ds(part * group, group)].reshape(group_rows, DH)
                frame_lane = WINDOW_LANE + part * group + (group_row >> 6)
                marks = jnp.where((group_lane < 3) | (group_lane == frame_lane), 1.0, 0.0)
                query = jnp.concatenate([query, marks.astype(jnp.bfloat16)], axis=1)
                keys = jnp.concatenate(
                    [k_time[...].reshape(length, DH), b_time[...].reshape(length, DH)], axis=1
                )
                scores = lax.dot_general(query, keys, NT, preferred_element_type=jnp.float32)
                weights, total = softmax_parts(scores)
                probs[slot, part] = weights
                inverse[slot, part] = jnp.broadcast_to(1.0 / total, (group_rows, DH))
                return carry

            lax.fori_loop(0, NF // group, rows_of, 0)

        return carry

    lax.fori_loop(0, SLOTS, weigh, 0)

    def give(slot, row, col, first, end):
        def one(index, carry):
            frame = peer(end - 1 - index)
            pltpu.make_async_remote_copy(
                src_ref=o_buf.at[slot, frame], dst_ref=out_ref.at[row, :, col],
                send_sem=send_sem.at[3], recv_sem=out_sem,
                device_id={"frame": frame}, device_id_type=MESH,
            ).start()
            return carry

        lax.fori_loop(0, end - first, one, 0)

    def mix(slot, carry):
        exists, row, col = owned(slot, me)

        @pl.when(exists)
        def _():
            got = s_got.at[slot]
            pltpu.make_async_copy(got, got, s_sem.at[slot]).wait()

            def rows_of(part, carry):
                values = s_got[slot].reshape(length, DH)
                mixed = jnp.dot(probs[slot, part], values, preferred_element_type=jnp.float32)
                temporal = (mixed * inverse[slot, part]).astype(jnp.bfloat16).astype(jnp.float32)
                for inside in range(group):
                    frame = part * group + inside
                    valid = token_valid(row, col, rows_ref[frame], cols_ref[frame])
                    both = temporal[inside * AREA : (inside + 1) * AREA] + s_got[slot, frame].astype(
                        jnp.float32
                    )
                    both = jnp.where(valid, both, 0.0).astype(jnp.bfloat16)
                    o_buf[slot, frame] = both.reshape(TS, TS, DH)
                return carry

            lax.fori_loop(0, NF // group, rows_of, 0)

            give(slot, row, col, NEAR + 1, NF)
            pltpu.make_async_copy(o_buf.at[slot, me], out_ref.at[row, :, col], out_sem).start()

        return carry

    lax.fori_loop(0, SLOTS, mix, 0)

    def give_near(slot, carry):
        exists, row, col = owned(slot, me)

        @pl.when(exists)
        def _():
            give(slot, row, col, 1, NEAR + 1)

        return carry

    lax.fori_loop(0, SLOTS, give_near, 0)

    pltpu.make_async_copy(out_ref, out_ref, out_sem).wait()
    exists, _, _ = owned(SLOTS - 1, me)

    def drain(owned_count):
        away = s_loc.at[pl.ds(0, tile_rows * tile_cols - owned_count)]
        for part in range(3):
            pltpu.make_async_copy(away, away, send_sem.at[part]).wait()
        sent = s_loc.at[pl.ds(0, owned_count * (NF - 1))]
        pltpu.make_async_copy(sent, sent, send_sem.at[3]).wait()

    @pl.when(exists)
    def _():
        drain(SLOTS)

    @pl.when(jnp.logical_not(exists))
    def _():
        drain(SLOTS - 1)


def per_device(queries, keys, values, back_reach, fwd_reach, valid_rows, valid_cols):
    _, token_rows, token_cols, _ = queries.shape
    tile_rows, tile_cols = token_rows // TS, token_cols // TS
    grid = (tile_rows, TS, tile_cols, TS, DH)
    padded = (tile_rows + 2, tile_cols + 2, AREA, DH)
    bf16 = jnp.bfloat16
    group = 4
    out = pl.pallas_call(
        kernel,
        out_shape=jax.ShapeDtypeStruct(grid, bf16),
        in_specs=[pl.BlockSpec(memory_space=pl.ANY)] * 7,
        out_specs=pl.BlockSpec(memory_space=pl.ANY),
        scratch_shapes=[
            pltpu.SMEM(back_reach.shape, jnp.int32),
            pltpu.SMEM(fwd_reach.shape, jnp.int32),
            pltpu.SMEM(valid_rows.shape, jnp.int32),
            pltpu.SMEM(valid_cols.shape, jnp.int32),
            pltpu.VMEM((tile_rows, tile_cols, TS, TS, DH), bf16),
            pltpu.VMEM((tile_rows, tile_cols, TS, TS, DH), bf16),
            pltpu.VMEM((tile_rows, tile_cols, TS, TS, DH), bf16),
            pltpu.VMEM(padded, bf16),
            pltpu.VMEM(padded, bf16),
            pltpu.VMEM(padded, bf16),
            pltpu.VMEM((tile_rows * tile_cols, AREA, DH), bf16),
            pltpu.VMEM((SLOTS, 2, NF, TS, TS, DH), bf16),
            pltpu.VMEM((SLOTS, NF, AREA, DH), bf16),
            pltpu.VMEM((NF, AREA, DH), bf16),
            pltpu.VMEM((NF, AREA, DH), bf16),
            pltpu.VMEM((SLOTS, NF // group, group * AREA, NF * AREA), bf16),
            pltpu.VMEM((SLOTS, NF // group, group * AREA, DH), jnp.float32),
            pltpu.VMEM((SLOTS, NF, TS, TS, DH), bf16),
            pltpu.SemaphoreType.DMA,
            pltpu.SemaphoreType.DMA((4,)),
            pltpu.SemaphoreType.REGULAR((STAGES - 1,)),
            pltpu.SemaphoreType.DMA((4,)),
            pltpu.SemaphoreType.DMA((SLOTS,)),
            pltpu.SemaphoreType.DMA((SLOTS,)),
            pltpu.SemaphoreType.DMA,
        ],
        compiler_params=pltpu.CompilerParams(
            collective_id=0, has_side_effects=True, vmem_limit_bytes=52 << 20
        ),
    )(
        *[
            pltpu.with_memory_space_constraint(array, pltpu.HBM)
            for array in (
                queries.reshape(grid), keys.reshape(grid), values.reshape(grid),
                back_reach, fwd_reach, valid_rows, valid_cols,
            )
        ]
    )
    return out.reshape(queries.shape)


def solution(mesh):
    in_specs = (
        P(("dp", "frame"), None, None, "row"),
        P(("dp", "frame"), None, None, "row"),
        P(("dp", "frame"), None, None, "row"),
        P("dp", None),
        P("dp", None),
        P("dp"),
        P("dp"),
    )
    out_specs = P(("dp", "frame"), None, None, "row")
    return jax.shard_map(
        per_device, mesh=mesh, in_specs=in_specs, out_specs=out_specs, check_vma=False
    )
```

```python
import math

import jax
import jax.numpy as jnp
from jax import lax
from jax.experimental import pallas as pl
from jax.experimental.pallas import tpu as pltpu
from jax.sharding import PartitionSpec as P

DH = 128
TS = 8
AREA = TS * TS
NF = 16
SLOTS = 4
WINDOW_LANE = 8
MASKED = -1e30
SCALE = math.log2(math.e) / math.sqrt(DH)
MESH = pl.DeviceIdType.MESH
NT = (((1,), (1,)), ((), ()))


def row_lane(rows):
    return (
        lax.broadcasted_iota(jnp.int32, (rows, DH), 0),
        lax.broadcasted_iota(jnp.int32, (rows, DH), 1),
    )


def token_valid(tile_row, tile_col, rows_ok, cols_ok):
    token, _ = row_lane(AREA)
    return (tile_row * TS + (token >> 3) < rows_ok) & (tile_col * TS + (token & 7) < cols_ok)


def key_bias(keys, valid):
    _, lane = row_lane(AREA)
    wide = keys.astype(jnp.float32)
    half = -0.5 * jnp.sum(wide * wide, axis=1, keepdims=True)
    high = half.astype(jnp.bfloat16).astype(jnp.float32)
    rest = half - high
    middle = rest.astype(jnp.bfloat16).astype(jnp.float32)
    low = rest - middle
    parts = jnp.where(lane == 0, high, jnp.where(lane == 1, middle, jnp.where(lane == 2, low, 0.0)))
    return jnp.where(valid, parts, jnp.where(lane == 0, MASKED, 0.0))


def softmax_parts(scores):
    highest = jnp.max(scores, axis=1, keepdims=True)
    weights = jnp.exp2((scores - highest) * SCALE)
    return weights.astype(jnp.bfloat16), jnp.sum(weights, axis=1, keepdims=True)


def kernel(
    q_hbm, k_hbm, v_hbm, back_hbm, fwd_hbm, rows_hbm, cols_hbm, out_ref,
    back_ref, fwd_ref, rows_ref, cols_ref,
    q_loc, k_loc, v_loc, k_pad, v_pad, b_pad, s_loc, qk_got, s_got, k_time, b_time, probs, inverse, o_buf,
    load_sem, small_sem, stage_sem, send_sem, qk_sem, s_sem, out_sem,
):
    tile_rows, _, tile_cols = q_hbm.shape[:3]
    me = lax.axis_index("frame")
    shift = 2 * lax.rem(lax.axis_index("row"), 2)
    barrier = pltpu.get_barrier_semaphore()

    def peer(step):
        half = (step + 1) // 2
        return lax.rem(me + jnp.where(lax.rem(step, 2) == 1, half, NF - half), NF)

    def owned(slot, owner):
        label = lax.rem(owner + shift, NF)
        last = slot == SLOTS - 1
        exists = jnp.logical_not(last & (lax.rem(label, 4) == 3))
        place = jnp.where(last, label - label // 4, label)
        tile = jnp.minimum(slot * NF + place, tile_rows * tile_cols - 1)
        return exists, tile // tile_cols, lax.rem(tile, tile_cols)

    def announce(semaphore):
        for neighbour in (peer(1), peer(2)):
            pl.semaphore_signal(
                semaphore, inc=1, device_id={"frame": neighbour}, device_id_type=MESH
            )

    announce(barrier)

    small = (
        (back_hbm, back_ref), (fwd_hbm, fwd_ref), (rows_hbm, rows_ref), (cols_hbm, cols_ref)
    )
    for index, (source, target) in enumerate(small):
        pltpu.make_async_copy(source, target, small_sem.at[index]).start()

    def load(col, carry):
        for source, target in ((q_hbm, q_loc), (k_hbm, k_loc), (v_hbm, v_loc)):
            pltpu.make_async_copy(source.at[:, :, col], target.at[:, col], load_sem).start()
        return carry

    lax.fori_loop(0, tile_cols, load, 0)

    def qk_copies(slot, row, col):
        for part, source in ((0, q_hbm), (1, k_hbm)):
            yield part, source.at[row, :, col], qk_got.at[slot, part, me]

    pl.semaphore_wait(barrier, 2)

    def send_qk(distance, carry):
        @pl.when(distance > 1)
        def _():
            pl.semaphore_wait(stage_sem.at[distance - 2], 2)

        @pl.when(distance < NF // 2)
        def _():
            announce(stage_sem.at[distance - 1])

        def send(index, carry):
            slot, side = index // 2, lax.rem(index, 2)
            owner = peer(2 * distance - 1 + side)
            exists, row, col = owned(slot, owner)

            @pl.when(exists & jnp.logical_not((distance == NF // 2) & (side == 1)))
            def _():
                for part, source, target in qk_copies(slot, row, col):
                    pltpu.make_async_remote_copy(
                        src_ref=source, dst_ref=target,
                        send_sem=send_sem.at[part], recv_sem=qk_sem.at[slot],
                        device_id={"frame": owner}, device_id_type=MESH,
                    ).start()

            return carry

        return lax.fori_loop(0, 2 * SLOTS, send, carry)

    lax.fori_loop(1, NF // 2 + 1, send_qk, 0)

    def keep_qk(slot, carry):
        exists, row, col = owned(slot, me)

        @pl.when(exists)
        def _():
            for _, source, target in qk_copies(slot, row, col):
                pltpu.make_async_copy(source, target, qk_sem.at[slot]).start()

        return carry

    lax.fori_loop(0, SLOTS, keep_qk, 0)

    nothing = jnp.zeros((AREA, DH), jnp.bfloat16)
    _, lane = row_lane(AREA)
    outside = jnp.where(lane == 0, MASKED, 0.0).astype(jnp.bfloat16)

    def border(row, col):
        k_pad[row, col] = nothing
        v_pad[row, col] = nothing
        b_pad[row, col] = outside

    def border_col(col, carry):
        border(0, col)
        border(tile_rows + 1, col)
        return carry

    def border_row(row, carry):
        border(row, 0)
        border(row, tile_cols + 1)
        return carry

    lax.fori_loop(0, tile_cols + 2, border_col, 0)
    lax.fori_loop(1, tile_rows + 1, border_row, 0)

    for _ in range(3):
        pltpu.make_async_copy(q_loc, q_loc, load_sem).wait()
    for index, (source, target) in enumerate(small):
        pltpu.make_async_copy(source, target, small_sem.at[index]).wait()

    rows_here, cols_here = rows_ref[me], cols_ref[me]

    def bias_tile(tile, carry):
        row, col = tile // tile_cols, lax.rem(tile, tile_cols)
        valid = token_valid(row, col, rows_here, cols_here)
        keys = k_loc[row, col].reshape(AREA, DH)
        k_pad[row + 1, col + 1] = keys
        v_pad[row + 1, col + 1] = v_loc[row, col].reshape(AREA, DH)
        b_pad[row + 1, col + 1] = key_bias(keys, valid).astype(jnp.bfloat16)
        return carry

    lax.fori_loop(0, tile_rows * tile_cols, bias_tile, 0)

    ones = jnp.where(lane < 3, 1.0, 0.0).astype(jnp.bfloat16)

    def near(ref, row, col):
        slabs = [ref[row + dy, pl.ds(col, 3)].reshape(3 * AREA, DH) for dy in range(3)]
        return jnp.concatenate(slabs, axis=0)

    def spatial(index, carry):
        slot, owner = index // NF, peer(NF - 1 - lax.rem(index, NF))
        exists, row, col = owned(slot, owner)

        @pl.when(exists)
        def _():
            tile = row * tile_cols + col
            query = jnp.concatenate([q_loc[row, col].reshape(AREA, DH), ones], axis=1)
            keys = jnp.concatenate([near(k_pad, row, col), near(b_pad, row, col)], axis=1)
            scores = lax.dot_general(query, keys, NT, preferred_element_type=jnp.float32)
            weights, total = softmax_parts(scores)
            mixed = jnp.dot(weights, near(v_pad, row, col), preferred_element_type=jnp.float32)
            valid = token_valid(row, col, rows_here, cols_here)
            s_loc[tile] = jnp.where(valid, mixed * (1.0 / total), 0.0).astype(jnp.bfloat16)
            target = s_got.at[slot, me]

            @pl.when(owner != me)
            def _():
                pltpu.make_async_remote_copy(
                    src_ref=s_loc.at[tile], dst_ref=target,
                    send_sem=send_sem.at[2], recv_sem=s_sem.at[slot],
                    device_id={"frame": owner}, device_id_type=MESH,
                ).start()

            @pl.when(owner == me)
            def _():
                pltpu.make_async_copy(s_loc.at[tile], target, s_sem.at[slot]).start()

        return carry

    lax.fori_loop(0, SLOTS * NF, spatial, 0)

    group = 4
    group_rows = group * AREA
    length = NF * AREA
    group_row, group_lane = row_lane(group_rows)

    def weigh(slot, carry):
        exists, row, col = owned(slot, me)

        @pl.when(exists)
        def _():
            got = qk_got.at[slot]
            pltpu.make_async_copy(got, got, qk_sem.at[slot]).wait()
            back, fwd = back_ref[row, col], fwd_ref[row, col]

            def bias_frame(frame, carry):
                valid = token_valid(row, col, rows_ref[frame], cols_ref[frame])
                keys = qk_got[slot, 1, frame].reshape(AREA, DH)
                bias = key_bias(keys, valid)
                gap = frame - (lane - WINDOW_LANE)
                window = (lane >= WINDOW_LANE) & (lane < WINDOW_LANE + NF)
                bias = jnp.where(window & ((gap < -back) | (gap > fwd)), MASKED, bias)
                k_time[frame] = keys
                b_time[frame] = bias.astype(jnp.bfloat16)
                return carry

            lax.fori_loop(0, NF, bias_frame, 0)

            def rows_of(part, carry):
                query = qk_got[slot, 0, pl.ds(part * group, group)].reshape(group_rows, DH)
                frame_lane = WINDOW_LANE + part * group + (group_row >> 6)
                marks = jnp.where((group_lane < 3) | (group_lane == frame_lane), 1.0, 0.0)
                query = jnp.concatenate([query, marks.astype(jnp.bfloat16)], axis=1)
                keys = jnp.concatenate(
                    [k_time[...].reshape(length, DH), b_time[...].reshape(length, DH)], axis=1
                )
                scores = lax.dot_general(query, keys, NT, preferred_element_type=jnp.float32)
                weights, total = softmax_parts(scores)
                probs[slot, part] = weights
                inverse[slot, part] = jnp.broadcast_to(1.0 / total, (group_rows, DH))
                return carry

            lax.fori_loop(0, NF // group, rows_of, 0)

        return carry

    lax.fori_loop(0, SLOTS, weigh, 0)

    def mix(slot, carry):
        exists, row, col = owned(slot, me)

        @pl.when(exists)
        def _():
            got = s_got.at[slot]
            pltpu.make_async_copy(got, got, s_sem.at[slot]).wait()

            def rows_of(part, carry):
                values = s_got[slot].reshape(length, DH)
                mixed = jnp.dot(probs[slot, part], values, preferred_element_type=jnp.float32)
                temporal = (mixed * inverse[slot, part]).astype(jnp.bfloat16).astype(jnp.float32)
                for inside in range(group):
                    frame = part * group + inside
                    valid = token_valid(row, col, rows_ref[frame], cols_ref[frame])
                    both = temporal[inside * AREA : (inside + 1) * AREA] + s_got[slot, frame].astype(
                        jnp.float32
                    )
                    both = jnp.where(valid, both, 0.0).astype(jnp.bfloat16)
                    o_buf[slot, frame] = both.reshape(TS, TS, DH)
                return carry

            lax.fori_loop(0, NF // group, rows_of, 0)

            def give(step, carry):
                frame = peer(NF - step)
                pltpu.make_async_remote_copy(
                    src_ref=o_buf.at[slot, frame], dst_ref=out_ref.at[row, :, col],
                    send_sem=send_sem.at[3], recv_sem=out_sem,
                    device_id={"frame": frame}, device_id_type=MESH,
                ).start()
                return carry

            lax.fori_loop(1, NF, give, 0)
            pltpu.make_async_copy(o_buf.at[slot, me], out_ref.at[row, :, col], out_sem).start()

        return carry

    lax.fori_loop(0, SLOTS, mix, 0)

    pltpu.make_async_copy(out_ref, out_ref, out_sem).wait()
    exists, _, _ = owned(SLOTS - 1, me)

    def drain(owned_count):
        away = s_loc.at[pl.ds(0, tile_rows * tile_cols - owned_count)]
        for part in range(3):
            pltpu.make_async_copy(away, away, send_sem.at[part]).wait()
        sent = s_loc.at[pl.ds(0, owned_count * (NF - 1))]
        pltpu.make_async_copy(sent, sent, send_sem.at[3]).wait()

    @pl.when(exists)
    def _():
        drain(SLOTS)

    @pl.when(jnp.logical_not(exists))
    def _():
        drain(SLOTS - 1)


def per_device(queries, keys, values, back_reach, fwd_reach, valid_rows, valid_cols):
    _, token_rows, token_cols, _ = queries.shape
    tile_rows, tile_cols = token_rows // TS, token_cols // TS
    grid = (tile_rows, TS, tile_cols, TS, DH)
    padded = (tile_rows + 2, tile_cols + 2, AREA, DH)
    bf16 = jnp.bfloat16
    group = 4
    out = pl.pallas_call(
        kernel,
        out_shape=jax.ShapeDtypeStruct(grid, bf16),
        in_specs=[pl.BlockSpec(memory_space=pl.ANY)] * 7,
        out_specs=pl.BlockSpec(memory_space=pl.ANY),
        scratch_shapes=[
            pltpu.SMEM(back_reach.shape, jnp.int32),
            pltpu.SMEM(fwd_reach.shape, jnp.int32),
            pltpu.SMEM(valid_rows.shape, jnp.int32),
            pltpu.SMEM(valid_cols.shape, jnp.int32),
            pltpu.VMEM((tile_rows, tile_cols, TS, TS, DH), bf16),
            pltpu.VMEM((tile_rows, tile_cols, TS, TS, DH), bf16),
            pltpu.VMEM((tile_rows, tile_cols, TS, TS, DH), bf16),
            pltpu.VMEM(padded, bf16),
            pltpu.VMEM(padded, bf16),
            pltpu.VMEM(padded, bf16),
            pltpu.VMEM((tile_rows * tile_cols, AREA, DH), bf16),
            pltpu.VMEM((SLOTS, 2, NF, TS, TS, DH), bf16),
            pltpu.VMEM((SLOTS, NF, AREA, DH), bf16),
            pltpu.VMEM((NF, AREA, DH), bf16),
            pltpu.VMEM((NF, AREA, DH), bf16),
            pltpu.VMEM((SLOTS, NF // group, group * AREA, NF * AREA), bf16),
            pltpu.VMEM((SLOTS, NF // group, group * AREA, DH), jnp.float32),
            pltpu.VMEM((SLOTS, NF, TS, TS, DH), bf16),
            pltpu.SemaphoreType.DMA,
            pltpu.SemaphoreType.DMA((4,)),
            pltpu.SemaphoreType.REGULAR((NF // 2 - 1,)),
            pltpu.SemaphoreType.DMA((4,)),
            pltpu.SemaphoreType.DMA((SLOTS,)),
            pltpu.SemaphoreType.DMA((SLOTS,)),
            pltpu.SemaphoreType.DMA,
        ],
        compiler_params=pltpu.CompilerParams(
            collective_id=0, has_side_effects=True, vmem_limit_bytes=52 << 20
        ),
    )(
        *[
            pltpu.with_memory_space_constraint(array, pltpu.HBM)
            for array in (
                queries.reshape(grid), keys.reshape(grid), values.reshape(grid),
                back_reach, fwd_reach, valid_rows, valid_cols,
            )
        ]
    )
    return out.reshape(queries.shape)


def solution(mesh):
    in_specs = (
        P(("dp", "frame"), None, None, "row"),
        P(("dp", "frame"), None, None, "row"),
        P(("dp", "frame"), None, None, "row"),
        P("dp", None),
        P("dp", None),
        P("dp"),
        P("dp"),
    )
    out_specs = P(("dp", "frame"), None, None, "row")
    return jax.shard_map(
        per_device, mesh=mesh, in_specs=in_specs, out_specs=out_specs, check_vma=False
    )
```
